512 devices in a mesh: dom: 64 (over z, y), src: 4 (over x), rel: 2 (over core).
Axes of the slice: x: 4, y: 4, z: 16, core: 2. Of those that a mesh axis runs over, the one named last changes fastest.
Arguments:
- source_feats: bfloat16 [131072, 256], P(('dom', 'src', 'rel')), may hold values from -6 to 6
- rel_weight: bfloat16 [12, 256, 256], P('rel'), may hold values from -0.375 to 0.375
- halo_pick: int32 [64, 4, 2, 64], P('dom', 'src', 'rel'), may hold values from 0 to 1
- entry_index: int32 [64, 4, 2, 3, 64], P('dom', 'src', 'rel'), may hold values from 0 to 63, as said below
- entry_count: int32 [64, 4, 2], P('dom', 'src', 'rel'), may hold values from 1 to 64, as said below
- entry_values: bfloat16 [64, 4, 2, 64, 128, 128], P('dom', 'src', 'rel'), may hold values from -0.125 to 0.125
- cotangent: bfloat16 [131072, 256], P(('dom', 'src', 'rel')), may hold values from -0.0546875 to 0.0546875
Outputs:
- out_feats: bfloat16 [131072, 256], P(('dom', 'src', 'rel'))
- grad_rel: float32 [12, 256, 256], P('rel')
The draws below stay inside these ranges and needn't reach their ends.
Inputs may be any that keep to these rules, and one draw needn't show every extreme that they name: `entry_index`: row 0 of an entry is a target block below 16, row 1 a partition below 64, row 2 a relation below 6. Over all 64 entries of one (p,s,g), every partition is named 64 // 64 times or once more. `entry_count`: live entries come first; some (p,s,g) has all 64 entries live in every draw.
All inputs are finite; a program needn't handle non-finite values.
Results may differ from the reference program's by a relative error of at most 0.0057.
Values may be sent and summed in bfloat16 or wider, within the bound.
A program may use at most 64 MiB of HBM per device.

```python
import jax
import jax.numpy as jnp
from jax import lax

D = 256
REL = 12
BLOCK = 128
SRC_BLOCKS = 2
NNZ = 64
PARTS_SIZE = 64
SRC_GROUPS = 4
REL_GROUPS = 2
REL_DEV = 6
TGT_BLOCKS = 16
TGT = 131072
SRC_ROWS = 131072
N_SRC = 4
N_REL = 2


def draw_entry_index(key, part):

    def one_device(device_key):
        keys = jax.random.split(device_key, 3)
        targets = jax.random.randint(keys[0], (NNZ,), 0, TGT_BLOCKS)
        peers = jax.random.permutation(keys[1], jnp.arange(NNZ, dtype=jnp.int32)) % PARTS_SIZE
        relations = jax.random.randint(keys[2], (NNZ,), 0, REL_DEV)
        return jnp.stack([targets, peers, relations]).astype(jnp.int32)
    keys = jax.random.split(jax.random.fold_in(key, 11), PARTS_SIZE * SRC_GROUPS * REL_GROUPS)
    table = jax.vmap(one_device)(keys)
    return table.reshape(PARTS_SIZE, SRC_GROUPS, REL_GROUPS, 3, NNZ)


def draw_entry_count(key, part):
    keys = jax.random.split(jax.random.fold_in(key, 23), 2)
    devices_all = PARTS_SIZE * SRC_GROUPS * REL_GROUPS
    counts = jax.random.randint(keys[0], (devices_all,), 1, NNZ + 1)
    full_device = jax.random.randint(keys[1], (), 0, devices_all)
    counts = counts.at[full_device].set(NNZ)
    return counts.reshape(PARTS_SIZE, SRC_GROUPS, REL_GROUPS).astype(jnp.int32)


def place_ends(result, own_key, low, top_value):
    index_at = [jax.random.randint(jax.random.fold_in(own_key, axis), (), 0, length) for axis, length in enumerate(result.shape)]
    widest = result.shape.index(max(result.shape))
    next_to = index_at[:widest] + [(index_at[widest] + 1) % result.shape[widest]] + index_at[widest + 1:]
    return result.at[tuple(index_at)].set(low).at[tuple(next_to)].set(top_value)


def block_levels(stream_key, extent, shards, least, largest):
    def one(dim, parts):
        steps = jax.random.uniform(jax.random.fold_in(jax.random.fold_in(stream_key, 6), dim), (parts,), jnp.float32, least / len(shards), largest / len(shards))
        return jnp.repeat(jnp.exp(steps), extent[dim] // parts).reshape((-1,) + (1,) * (len(extent) - dim - 1))

    factor_of = one(*shards[0])
    for cut in shards[1:]:
        factor_of = factor_of * one(*cut)
    return factor_of


def noise(key, dims, width, limit, cuts=(), kind=jnp.bfloat16):
    entries = jax.random.normal(key, dims, jnp.float32) * width
    if len(cuts) > 0:
        entries = block_levels(key, dims, cuts, -0.22, 0.18) * entries
    return jnp.clip(entries, min=-limit, max=limit).astype(kind)


def setup_inputs(seed: int = 0) -> dict:
    key_list = jax.random.split(jax.random.key(seed), 8)
    source_feats = noise(key_list[0], (SRC_ROWS, D), 1.0, 6.0, ((0, 512),))
    rel_weight = noise(key_list[1], (REL, D, D), D ** -0.5, 0.375, ((0, 2),))
    halo_pick = place_ends(jax.random.randint(key_list[2], (PARTS_SIZE, SRC_GROUPS, REL_GROUPS, PARTS_SIZE), 0, SRC_BLOCKS), jax.random.fold_in(key_list[2], 1), 0, SRC_BLOCKS - 1).astype(jnp.int32)
    entry_index = draw_entry_index(jax.random.fold_in(key_list[7], 71), 0)
    entry_count = draw_entry_count(jax.random.fold_in(key_list[7], 71), 0)
    entry_values = noise(key_list[5], (PARTS_SIZE, SRC_GROUPS, REL_GROUPS, NNZ, BLOCK, BLOCK), ((TGT_BLOCKS / (0.5 * BLOCK * NNZ * N_SRC * N_REL)) ** 0.5), 0.125, ((0, 64), (1, 4), (2, 2)))
    cotangent = noise(key_list[6], (TGT, D), ((REL / TGT) ** 0.5), 0.0546875, ((0, 512),))
    return dict(source_feats=source_feats, rel_weight=rel_weight, halo_pick=halo_pick, entry_index=entry_index, entry_count=entry_count, entry_values=entry_values, cotangent=cotangent)


def silu_slope(pre_values):
    logistic = jax.nn.sigmoid(pre_values)
    return logistic * (1.0 + pre_values * (1.0 - logistic))


def reference(source_feats, rel_weight, halo_pick, entry_index, entry_count, entry_values, cotangent):
    source_view = source_feats.reshape(PARTS_SIZE, SRC_GROUPS, REL_GROUPS, SRC_BLOCKS, BLOCK, D)
    grouped_weight = rel_weight.reshape(REL_GROUPS, REL_DEV, D, D).astype(jnp.float32)
    cotangent_view = cotangent.reshape(PARTS_SIZE, TGT_BLOCKS * BLOCK, D)
    peer_index = jnp.arange(PARTS_SIZE, dtype=jnp.int32)
    entry_number = jnp.arange(NNZ, dtype=jnp.int32)
    highest = lax.Precision.HIGHEST

    def one_partition(grad_total, inputs):
        chosen, entry_table, live_count, values, cotangent_rows = inputs
        pre_sum = jnp.zeros((TGT_BLOCKS * BLOCK, D), jnp.float32)
        merged_groups = []
        for group in range(REL_GROUPS):
            merged = jnp.zeros((REL_DEV, TGT_BLOCKS * BLOCK, D), jnp.float32)
            for panel in range(SRC_GROUPS):
                halo_blocks = source_view[:, panel, group][peer_index, chosen[panel, group]]
                table = entry_table[panel, group]
                picked = halo_blocks[table[1]]
                messages = jnp.einsum("eij,ejd->eid", values[panel, group].astype(jnp.float32),
                                      picked.astype(jnp.float32), precision=highest)
                live_mask = (entry_number < live_count[panel, group]).astype(jnp.float32)
                messages = messages * live_mask[:, None, None]
                segment_ids = (table[2] * TGT_BLOCKS + table[0]).astype(jnp.int32)
                sums = jax.ops.segment_sum(messages, segment_ids, num_segments=REL_DEV * TGT_BLOCKS)
                relation_terms = lax.optimization_barrier(sums.astype(jnp.bfloat16))
                merged = merged + relation_terms.astype(jnp.float32).reshape(REL_DEV, TGT_BLOCKS * BLOCK, D)
            pre_sum = pre_sum + jnp.einsum("rtd,rde->te", merged, grouped_weight[group], precision=highest)
            merged_groups.append(merged)
        out_rows = jax.nn.silu(pre_sum).astype(jnp.bfloat16)
        grad_pre = lax.optimization_barrier((cotangent_rows.astype(jnp.float32) * silu_slope(pre_sum)).astype(jnp.bfloat16))
        grad_float = grad_pre.astype(jnp.float32)
        weight_terms = jnp.stack([jnp.einsum("rtd,te->rde", merged, grad_float, precision=highest)
                                  for merged in merged_groups])
        return grad_total + weight_terms, out_rows

    start_total = jnp.zeros((REL_GROUPS, REL_DEV, D, D), jnp.float32)
    grad_total, out_rows = lax.scan(one_partition, start_total,
                                    (halo_pick, entry_index, entry_count, entry_values, cotangent_view))
    return out_rows.reshape(TGT, D), grad_total.reshape(REL, D, D)
```

```python
import jax
import jax.numpy as jnp
from jax import lax
from jax.experimental import pallas as pl
from jax.experimental.pallas import tpu as pltpu
from jax.sharding import PartitionSpec as P

MESH = pl.DeviceIdType.MESH
F32 = jnp.float32
BF16 = jnp.bfloat16

NY = 4
NZ = 16
NX = 4
BLOCK = 128
D = 256
REL = 6
CHUNKS = 8
ROWS_P = 160
HALF_P = 80
ROWS_Q = 96
HALF_Q = 48


def remote(src, dst, send_sem, recv_sem, to):
    return pltpu.make_async_remote_copy(
        src_ref=src, dst_ref=dst, send_sem=send_sem, recv_sem=recv_sem,
        device_id=to, device_id_type=MESH)


def signal_all(targets):
    barrier = pltpu.get_barrier_semaphore()
    for to in targets:
        pl.semaphore_signal(barrier, inc=1, device_id=to, device_id_type=MESH)
    pl.semaphore_wait(barrier, len(targets))


def gather_kernel(src, out, own_sem, pf_s, pf_r, pb_s, pb_r, yf_s, yf_r, yb_s, yb_r,
                  ff_s, ff_r, fb_s, fb_r, q0_s, q0_r, qf_s, qf_r, qb_s, qb_r):
    dom = lax.axis_index("dom")
    z, y = dom // NY, dom % NY

    def at(zo, yo):
        return ((z + zo + NZ) % NZ) * NY + (y + yo + NY) % NY

    z_up, z_down = {"dom": at(1, 0)}, {"dom": at(-1, 0)}
    y_up, y_down, y_far = {"dom": at(0, 1)}, {"dom": at(0, -1)}, {"dom": at(0, 2)}
    signal_all([z_up, z_down, y_up, y_down, y_far])

    sent = []

    def send(where, row, count, s, r, to):
        index = at(*where)
        own = where == (0, 0)
        source = src.at[pl.ds(row, count)] if own else out.at[index, pl.ds(row, count)]
        copy = remote(source, out.at[index, pl.ds(row, count)], s, r, to)
        copy.start()
        sent.append(copy)

    def arrive(where, row, count, s, r):
        index = at(*where)
        ref = out.at[index, pl.ds(row, count)]
        remote(ref, ref, s, r, z_up).wait_recv()

    own_copy = pltpu.make_async_copy(src, out.at[dom], own_sem)

    def p_step(k):
        lo, n = (0, ROWS_P) if k < NZ // 2 else (0, HALF_P)
        send((-(k - 1), 0), lo, n, pf_s.at[k], pf_r.at[k], z_up)
        lo, n = (0, ROWS_P) if k < NZ // 2 else (HALF_P, HALF_P)
        send((k - 1, 0), lo, n, pb_s.at[k], pb_r.at[k], z_down)

    def p_arrive(k):
        lo, n = (0, ROWS_P) if k < NZ // 2 else (0, HALF_P)
        arrive((-k, 0), lo, n, pf_s.at[k], pf_r.at[k])
        lo, n = (0, ROWS_P) if k < NZ // 2 else (HALF_P, HALF_P)
        arrive((k, 0), lo, n, pb_s.at[k], pb_r.at[k])

    def q_step(k, m):
        lo, n = (ROWS_P, ROWS_Q) if k < NZ // 2 else (ROWS_P, HALF_Q)
        send((-(k - 1), m), lo, n, qf_s.at[k, m], qf_r.at[k, m], z_up)
        lo, n = (ROWS_P, ROWS_Q) if k < NZ // 2 else (ROWS_P + HALF_Q, HALF_Q)
        send((k - 1, m), lo, n, qb_s.at[k, m], qb_r.at[k, m], z_down)

    def q_arrive(k, m):
        lo, n = (ROWS_P, ROWS_Q) if k < NZ // 2 else (ROWS_P, HALF_Q)
        arrive((-k, m), lo, n, qf_s.at[k, m], qf_r.at[k, m])
        lo, n = (ROWS_P, ROWS_Q) if k < NZ // 2 else (ROWS_P + HALF_Q, HALF_Q)
        arrive((k, m), lo, n, qb_s.at[k, m], qb_r.at[k, m])

    def offsets(k):
        if k == 0:
            return [(0, 0)]
        if k == NZ // 2:
            return [(2 * k - 1, k)]
        return [(2 * k - 1, -k), (2 * k, k)]

    def y_step(k):
        for j, zo in offsets(k):
            send((zo, 0), 0, ROWS_P, yf_s.at[j], yf_r.at[j], y_up)
            send((zo, 0), 0, ROWS_P, yb_s.at[j], yb_r.at[j], y_down)

    def y_forward(k):
        for j, zo in offsets(k):
            arrive((zo, -1), 0, ROWS_P, yf_s.at[j], yf_r.at[j])
            send((zo, -1), 0, HALF_P, ff_s.at[j], ff_r.at[j], y_up)
            arrive((zo, 1), 0, ROWS_P, yb_s.at[j], yb_r.at[j])
            send((zo, 1), HALF_P, HALF_P, fb_s.at[j], fb_r.at[j], y_down)

    p_step(1)
    send((0, 0), ROWS_P, ROWS_Q, q0_s.at[0], q0_r.at[0], y_up)
    send((0, 0), ROWS_P, ROWS_Q, q0_s.at[1], q0_r.at[1], y_down)
    send((0, 0), ROWS_P, ROWS_Q, q0_s.at[2], q0_r.at[2], y_far)
    q_step(1, 0)
    y_step(0)
    own_copy.start()
    arrive((0, -1), ROWS_P, ROWS_Q, q0_s.at[0], q0_r.at[0])
    q_step(1, 3)
    arrive((0, 1), ROWS_P, ROWS_Q, q0_s.at[1], q0_r.at[1])
    q_step(1, 1)
    arrive((0, 2), ROWS_P, ROWS_Q, q0_s.at[2], q0_r.at[2])
    q_step(1, 2)
    for k in range(1, NZ // 2 + 1):
        p_arrive(k)
        if k < NZ // 2:
            p_step(k + 1)
        y_step(k)
        y_forward(k - 1)
        for m in (0, 3, 1, 2):
            q_arrive(k, m)
            if k < NZ // 2:
                q_step(k + 1, m)
    y_forward(NZ // 2)
    for k in range(NZ // 2 + 1):
        for j, zo in offsets(k):
            arrive((zo, 2), 0, HALF_P, ff_s.at[j], ff_r.at[j])
            arrive((zo, 2), HALF_P, HALF_P, fb_s.at[j], fb_r.at[j])
    for copy in sent:
        copy.wait_send()
    own_copy.wait()


def gather_sources(source_feats):
    rows = source_feats.shape[0]
    dma = pltpu.SemaphoreType.DMA
    steps = NZ // 2 + 1
    return pl.pallas_call(
        gather_kernel,
        out_shape=jax.ShapeDtypeStruct((NZ * NY, rows, D), BF16),
        in_specs=[pl.BlockSpec(memory_space=pltpu.VMEM)],
        out_specs=pl.BlockSpec(memory_space=pl.ANY),
        scratch_shapes=[dma] + [dma((steps,))] * 4 + [dma((NZ,))] * 8
        + [dma((3,))] * 2 + [dma((steps, NY))] * 4,
        compiler_params=pltpu.CompilerParams(collective_id=0, has_side_effects=True),
        name="gather_sources",
    )(source_feats)


def message_kernel(pick, table, count, blocks, values, weight, terms_out, pre_out,
                   held, total, terms, held_sem, terms_sem):
    live = count[0]

    def fetch(e):
        q = table[1, e]
        return pltpu.make_async_copy(blocks.at[2 * q + pick[q]], held.at[e], held_sem.at[e])

    def start(e, carry):
        fetch(e).start()
        return carry

    lax.fori_loop(0, live, start, 0)

    def clear(i, carry):
        total[i] = jnp.zeros((BLOCK, D), F32)
        return carry

    lax.fori_loop(0, CHUNKS * REL * 2, clear, 0)

    def step(e, carry):
        fetch(e).wait()
        message = jnp.dot(values[e], held[e], preferred_element_type=F32)
        target = table[0, e]
        slot = (target // 2 * REL + table[2, e]) * 2 + target % 2
        total[slot] = total[slot] + message
        return carry

    lax.fori_loop(0, live, step, 0)

    def flush(c):
        return pltpu.make_async_copy(terms.at[c], terms_out.at[c], terms_sem.at[c])

    def project(c, carry):
        for r in range(REL):
            for h in range(2):
                terms[c, r, pl.ds(h * BLOCK, BLOCK)] = total[(c * REL + r) * 2 + h].astype(BF16)
        flush(c).start()
        value = jnp.dot(terms[c, 0], weight[0], preferred_element_type=F32)
        for r in range(1, REL):
            value = value + jnp.dot(terms[c, r], weight[r], preferred_element_type=F32)
        pre_out[c] = value
        return carry

    lax.fori_loop(0, CHUNKS, project, 0)
    for c in range(CHUNKS):
        flush(c).wait()


def messages(pick, table, count, blocks, values, weight):
    smem = pl.BlockSpec(memory_space=pltpu.SMEM)
    vmem = pl.BlockSpec(memory_space=pltpu.VMEM)
    entries = values.shape[0]
    return pl.pallas_call(
        message_kernel,
        out_shape=(jax.ShapeDtypeStruct((CHUNKS, REL, 2 * BLOCK, D), BF16),
                   jax.ShapeDtypeStruct((CHUNKS, 2 * BLOCK, D), F32)),
        in_specs=[smem, smem, smem, pl.BlockSpec(memory_space=pl.ANY), vmem, vmem],
        out_specs=(pl.BlockSpec(memory_space=pl.ANY), vmem),
        scratch_shapes=[
            pltpu.VMEM((entries, BLOCK, D), BF16),
            pltpu.VMEM((CHUNKS * REL * 2, BLOCK, D), F32),
            pltpu.VMEM((CHUNKS, REL, 2 * BLOCK, D), BF16),
            pltpu.SemaphoreType.DMA((entries,)),
            pltpu.SemaphoreType.DMA((CHUNKS,)),
        ],
        compiler_params=pltpu.CompilerParams(vmem_limit_bytes=56 << 20),
        name="messages",
    )(pick, table, count, blocks, values, weight)


def reduce_kernel(pre, terms_hbm, cot, out, grad,
                  ex, cs, cr, rows, terms, acc,
                  a_send, a_recv, b_send, b_recv, a_sum, b_sum,
                  a2_send, a2_recv, b2_send, b2_recv, tail, z_send, z_recv, z_full,
                  a_all, b_all,
                  t_sem, ex_s, ex_r, cx_s, cx_r, gx_s, gx_r, gp_s, gp_r,
                  s1_s, s1_r, s2_s, s2_r, z1_s, z1_r, z2_s, z2_r, s4_s, s4_r, s5_s, s5_r):
    dom, s, g = lax.axis_index("dom"), lax.axis_index("src"), lax.axis_index("rel")
    z, y = dom // NY, dom % NY
    partner = {"rel": 1 - g}

    def x_peer(d):
        return {"src": (s + d) % NX}

    def y_peer(d):
        return {"dom": z * NY + (y + d) % NY}

    def z_peer(d):
        return {"dom": ((z + d) % NZ) * NY + y}

    signal_all([partner] + [x_peer(d) for d in range(1, NX)]
               + [y_peer(d) for d in range(1, NY)] + [z_peer(d) for d in range(1, NZ)])

    sent = []

    def go(copy):
        copy.start()
        sent.append(copy)
        return copy

    swaps = {}
    for i in (1, 2, 3, 0):
        sp = (s + i) % NX
        swaps[i] = go(remote(pre.at[sp * 2 + (1 - g)], ex.at[sp], ex_s.at[i], ex_r.at[i], partner))
    load = pltpu.make_async_copy(terms_hbm, terms, t_sem)
    load.start()
    z_send[...] = jnp.zeros_like(z_send)

    moves = {}
    for i in (1, 2, 3):
        sp = (s + i) % NX
        swaps[i].wait_recv()
        for b in range(8):
            part = pl.ds(b * 32, 32)
            cs[i - 1, part] = (pre[sp * 2 + g, part] + ex[sp, part]).astype(BF16)
        moves[i] = go(remote(cs.at[i - 1], cr.at[i - 1], cx_s.at[i - 1], cx_r.at[i - 1], x_peer(i)))
    swaps[0].wait_recv()
    for i in (1, 2, 3):
        moves[i].wait_recv()
    own = s * 2 + g
    for b in range(8):
        part = pl.ds(b * 32, 32)
        value = pre[own, part] + ex[s, part]
        for i in range(3):
            value = value + cr[i, part].astype(F32)
        logistic = 1.0 / (1.0 + jnp.exp(-value))
        out[part] = (value * logistic).astype(BF16)
        slope = logistic * (1.0 + value * (1.0 - logistic))
        rows[own, part] = (cot[part].astype(F32) * slope).astype(BF16)

    gx = {}
    for d in (1, 2, 3):
        gx[d] = go(remote(rows.at[own], rows.at[own], gx_s.at[d], gx_r.at[d], x_peer(d)))
    gp = {0: go(remote(rows.at[own], rows.at[own], gp_s.at[0], gp_r.at[0], partner))}

    def add_terms(c, first=False):
        def one(r, carry):
            product = lax.dot_general(terms[c, r], rows[c], (((0,), (0,)), ((), ())),
                                      preferred_element_type=F32)
            if first:
                acc[r] = product
            else:
                acc[r] = acc[r] + product
            return carry

        lax.fori_loop(0, REL, one, 0)

    load.wait()
    add_terms(own, first=True)
    gp[0].wait_recv()
    add_terms(s * 2 + 1 - g)
    for d in (1, 2, 3):
        gx[d].wait_recv()
        c = (s - d + NX) % NX * 2 + g
        gp[d] = go(remote(rows.at[c], rows.at[c], gp_s.at[d], gp_r.at[d], partner))
        add_terms(c)
    for d in (1, 2, 3):
        gp[d].wait_recv()
        add_terms((s - d + NX) % NX * 2 + 1 - g)

    first_a, first_b = {}, {}
    for d in (1, 2, 3):
        xp, yp = (s + d) % NX, (y + d) % NY
        for r in range(3):
            a_send[d - 1, r] = acc[r, pl.ds(xp * 64, 64)].astype(BF16)
        first_a[d] = go(remote(a_send.at[d - 1], a_recv.at[d - 1], s1_s.at[0, d], s1_r.at[0, d], x_peer(d)))
        for r in range(3):
            b_send[d - 1, r] = acc[3 + r, pl.ds(yp * 64, 64)].astype(BF16)
        first_b[d] = go(remote(b_send.at[d - 1], b_recv.at[d - 1], s1_s.at[1, d], s1_r.at[1, d], y_peer(d)))
    for d in (1, 2, 3):
        first_a[d].wait_recv()
        first_b[d].wait_recv()
    for r in range(3):
        value = acc[r, pl.ds(s * 64, 64)]
        for i in range(3):
            value = value + a_recv[i, r].astype(F32)
        a_sum[r] = value
        value = acc[3 + r, pl.ds(y * 64, 64)]
        for i in range(3):
            value = value + b_recv[i, r].astype(F32)
        b_sum[r] = value
    second_a, second_b = {}, {}
    for d in (1, 2, 3):
        xp, yp = (s + d) % NX, (y + d) % NY
        for r in range(3):
            a2_send[d - 1, r] = a_sum[r, pl.ds(yp * 16, 16)].astype(BF16)
        second_a[d] = go(remote(a2_send.at[d - 1], a2_recv.at[d - 1], s2_s.at[0, d], s2_r.at[0, d], y_peer(d)))
        for r in range(3):
            b2_send[d - 1, r] = b_sum[r, pl.ds(xp * 16, 16)].astype(BF16)
        second_b[d] = go(remote(b2_send.at[d - 1], b2_recv.at[d - 1], s2_s.at[1, d], s2_r.at[1, d], x_peer(d)))
    for d in (1, 2, 3):
        second_a[d].wait_recv()
        second_b[d].wait_recv()
    for r in range(3):
        value = a_sum[r, pl.ds(y * 16, 16)]
        for i in range(3):
            value = value + a2_recv[i, r].astype(F32)
        tail[r] = value
        value = b_sum[r, pl.ds(s * 16, 16)]
        for i in range(3):
            value = value + b2_recv[i, r].astype(F32)
        tail[3 + r] = value
    for j in range(NZ):
        for r in range(REL):
            z_send[j, pl.ds(r, 1)] = tail[r, pl.ds(j, 1)]
    third = []
    for d in range(1, NZ):
        third.append(go(remote(z_send.at[(z + d) % NZ], z_recv.at[d], z1_s.at[d], z1_r.at[d], z_peer(d))))
    value = z_send[z]
    for d in range(1, NZ):
        third[d - 1].wait_recv()
        value = value + z_recv[d]
    z_full[z] = value

    fourth = []
    for d in range(1, NZ):
        fourth.append(go(remote(z_full.at[z], z_full.at[z], z2_s.at[d], z2_r.at[d], z_peer(d))))
    for copy in fourth:
        copy.wait_recv()
    for j in range(NZ):
        for r in range(REL):
            tail[r, pl.ds(j, 1)] = z_full[j, pl.ds(r, 1)]
    for r in range(3):
        a_all[s, y, r] = tail[r].astype(BF16)
        b_all[y, s, r] = tail[3 + r].astype(BF16)
    fifth = []
    for d in (1, 2, 3):
        fifth.append(go(remote(a_all.at[s, y], a_all.at[s, y], s4_s.at[0, d], s4_r.at[0, d], y_peer(d))))
        fifth.append(go(remote(b_all.at[y, s], b_all.at[y, s], s4_s.at[1, d], s4_r.at[1, d], x_peer(d))))
    for copy in fifth:
        copy.wait_recv()
    sixth = []
    for d in (1, 2, 3):
        sixth.append(go(remote(a_all.at[s], a_all.at[s], s5_s.at[0, d], s5_r.at[0, d], x_peer(d))))
        sixth.append(go(remote(b_all.at[y], b_all.at[y], s5_s.at[1, d], s5_r.at[1, d], y_peer(d))))
    for copy in sixth:
        copy.wait_recv()
    for i in range(4):
        for j in range(4):
            for r in range(3):
                part = pl.ds(64 * i + 16 * j, 16)
                grad[r, part] = a_all[i, j, r].astype(F32)
                grad[3 + r, part] = b_all[i, j, r].astype(F32)
    for copy in sent:
        copy.wait_send()


def reduce_and_grad(pre, terms, cotangent):
    vmem = pl.BlockSpec(memory_space=pltpu.VMEM)
    dma = pltpu.SemaphoreType.DMA
    V = pltpu.VMEM
    return pl.pallas_call(
        reduce_kernel,
        out_shape=(jax.ShapeDtypeStruct((2 * BLOCK, D), BF16),
                   jax.ShapeDtypeStruct((REL, D, D), F32)),
        in_specs=[vmem, pl.BlockSpec(memory_space=pl.ANY), vmem],
        out_specs=(vmem, vmem),
        scratch_shapes=[
            V((NX, 256, D), F32), V((3, 256, D), BF16), V((3, 256, D), BF16),
            V((CHUNKS, 256, D), BF16), V((CHUNKS, REL, 256, D), BF16), V((REL, D, D), F32),
            V((3, 3, 64, D), BF16), V((3, 3, 64, D), BF16), V((3, 3, 64, D), BF16), V((3, 3, 64, D), BF16),
            V((3, 64, D), F32), V((3, 64, D), F32),
            V((3, 3, 16, D), BF16), V((3, 3, 16, D), BF16), V((3, 3, 16, D), BF16), V((3, 3, 16, D), BF16),
            V((REL, 16, D), F32), V((NZ, 8, D), F32), V((NZ, 8, D), F32), V((NZ, 8, D), F32),
            V((4, 4, 3, 16, D), BF16), V((4, 4, 3, 16, D), BF16),
            dma, dma((4,)), dma((4,)), dma((3,)), dma((3,)), dma((4,)), dma((4,)), dma((4,)), dma((4,)),
            dma((2, 4)), dma((2, 4)), dma((2, 4)), dma((2, 4)), dma((NZ,)), dma((NZ,)), dma((NZ,)), dma((NZ,)),
            dma((2, 4)), dma((2, 4)), dma((2, 4)), dma((2, 4)),
        ],
        compiler_params=pltpu.CompilerParams(
            collective_id=1, has_side_effects=True, vmem_limit_bytes=56 << 20),
        name="reduce_and_grad",
    )(pre, terms, cotangent)


def local(source_feats, rel_weight, halo_pick, entry_index, entry_count, entry_values, cotangent):
    slots = entry_index.shape[-1]
    gathered = gather_sources(source_feats)
    terms, pre = messages(
        halo_pick.reshape(-1), entry_index.reshape(3, slots), entry_count.reshape(1),
        gathered.reshape(-1, BLOCK, D), entry_values.reshape(slots, BLOCK, BLOCK), rel_weight)
    return reduce_and_grad(pre, terms, cotangent)


def solution(mesh):
    return jax.shard_map(
        local,
        mesh=mesh,
        in_specs=(
            P(("dom", "src", "rel"), None),
            P("rel", None, None),
            P("dom", "src", "rel", None),
            P("dom", "src", "rel", None, None),
            P("dom", "src", "rel"),
            P("dom", "src", "rel", None, None, None),
            P(("dom", "src", "rel"), None),
        ),
        out_specs=(P(("dom", "src", "rel"), None), P("rel", None, None)),
        check_vma=False,
    )
```

```python
import jax
import jax.numpy as jnp
from jax import lax
from jax.experimental import pallas as pl
from jax.experimental.pallas import tpu as pltpu
from jax.sharding import PartitionSpec as P

MESH = pl.DeviceIdType.MESH
F32 = jnp.float32
BF16 = jnp.bfloat16
I32 = jnp.int32

NY = 4
NZ = 16
NX = 4
PARTS = 64
BLOCK = 128
D = 256
REL = 6
CHUNKS = 8
SLOTS = CHUNKS * REL * 2
ROWS_P = 160
HALF_P = 80
ROWS_Q = 96
HALF_Q = 48
FAR = NZ // 2

TIME_P = [0.0] + [4.0 * k for k in range(1, 9)]
TIME_Y = [3.0, 8.0, 13.2, 18.5, 24.0, 29.0, 34.5, 39.7, 44.0]
TIME_Q = [0.0, 7.5, 15.0, 22.5, 30.0, 35.0, 39.0, 43.0, 45.0]


def remote(src, dst, send_sem, recv_sem, to):
    return pltpu.make_async_remote_copy(
        src_ref=src, dst_ref=dst, send_sem=send_sem, recv_sem=recv_sem,
        device_id=to, device_id_type=MESH)


def offsets(k):
    if k == 0:
        return [(0, 0)]
    if k == FAR:
        return [(2 * k - 1, k)]
    return [(2 * k - 1, -k), (2 * k, k)]


def layer_kernel(src, table, pick, count, values_hbm, weight_hbm, cot,
                 out, a_out, b_out,
                 held, values, weight, chain, tab, tab_s, terms, work, keep, give, ex, cs, cr, rows, acc,
                 result, a_all, b_all,
                 a_send, a_recv, b_send, b_recv, a_sum, b_sum,
                 a2_send, a2_recv, b2_send, b2_recv, tail, z_rows, z_send, z_recv, z_full,
                 own_sem, val_sem, w_sem, tab_sem, out_sem,
                 pf_s, pf_r, pb_s, pb_r, yf_s, yf_r, yb_s, yb_r,
                 ff_s, ff_r, fb_s, fb_r, q0_s, q0_r, qf_s, qf_r, qb_s, qb_r,
                 ex_s, ex_r, cx_s, cx_r, gx_s, gx_r, gp_s, gp_r,
                 s1_s, s1_r, s2_s, s2_r, z1_s, z1_r, z2_s, z2_r, s4_s, s4_r, s5_s, s5_r):
    dom, s, g = lax.axis_index("dom"), lax.axis_index("src"), lax.axis_index("rel")
    z, y = dom // NY, dom % NY
    turn = 1 - 2 * g
    partner = {"rel": 1 - g}

    def at(zo, yo):
        return ((z + zo + NZ) % NZ) * NY + (y + yo + NY) % NY

    def x_at(o):
        return (s + o + NX) % NX

    def y_at(o):
        return (y + o + NY) % NY

    def x_dev(o):
        return {"src": x_at(o)}

    def y_dev(o):
        return {"dom": z * NY + y_at(o)}

    def z_dev(o):
        return {"dom": ((z + o + NZ) % NZ) * NY + y}

    own_copy = pltpu.make_async_copy(src, held.at[dom], own_sem)
    own_copy.start()
    val_copy = pltpu.make_async_copy(values_hbm, values, val_sem)
    val_copy.start()
    w_copy = pltpu.make_async_copy(weight_hbm, weight, w_sem)
    w_copy.start()

    near = [partner, x_dev(1), x_dev(-1), y_dev(1), y_dev(-1), y_dev(2), z_dev(1), z_dev(-1)]
    barrier = pltpu.get_barrier_semaphore()
    for to in near:
        pl.semaphore_signal(barrier, inc=1, device_id=to, device_id_type=MESH)
    own_copy.wait()
    pl.semaphore_wait(barrier, len(near))

    sent = []

    def go(copy):
        copy.start()
        sent.append(copy)
        return copy

    def send(where, row, n, s_sem, r_sem, to):
        ref = held.at[at(*where), pl.ds(row, n)]
        go(remote(ref, ref, s_sem, r_sem, to))

    def arrive(where, row, n, s_sem, r_sem):
        ref = held.at[at(*where), pl.ds(row, n)]
        remote(ref, ref, s_sem, r_sem, z_dev(1)).wait_recv()

    def cut(k, low, full, half, back):
        if k < FAR:
            return low, full
        return low + (half if back else 0), half

    def p_step(k):
        send((-(k - 1), 0), *cut(k, 0, ROWS_P, HALF_P, False), pf_s.at[k], pf_r.at[k], z_dev(1))
        send((k - 1, 0), *cut(k, 0, ROWS_P, HALF_P, True), pb_s.at[k], pb_r.at[k], z_dev(-1))

    def p_arrive(k):
        arrive((-k, 0), *cut(k, 0, ROWS_P, HALF_P, False), pf_s.at[k], pf_r.at[k])
        arrive((k, 0), *cut(k, 0, ROWS_P, HALF_P, True), pb_s.at[k], pb_r.at[k])

    def q_step(k, m):
        send((-(k - 1), m), *cut(k, ROWS_P, ROWS_Q, HALF_Q, False), qf_s.at[k, m], qf_r.at[k, m], z_dev(1))
        send((k - 1, m), *cut(k, ROWS_P, ROWS_Q, HALF_Q, True), qb_s.at[k, m], qb_r.at[k, m], z_dev(-1))

    def q_arrive(k, m):
        arrive((-k, m), *cut(k, ROWS_P, ROWS_Q, HALF_Q, False), qf_s.at[k, m], qf_r.at[k, m])
        arrive((k, m), *cut(k, ROWS_P, ROWS_Q, HALF_Q, True), qb_s.at[k, m], qb_r.at[k, m])

    def y_step(k):
        for j, zo in offsets(k):
            send((zo, 0), 0, ROWS_P, yf_s.at[j], yf_r.at[j], y_dev(1))
            send((zo, 0), 0, ROWS_P, yb_s.at[j], yb_r.at[j], y_dev(-1))

    def y_forward(k):
        for j, zo in offsets(k):
            arrive((zo, -1), 0, ROWS_P, yf_s.at[j], yf_r.at[j])
            send((zo, -1), 0, HALF_P, ff_s.at[j], ff_r.at[j], y_dev(1))
            arrive((zo, 1), 0, ROWS_P, yb_s.at[j], yb_r.at[j])
            send((zo, 1), HALF_P, HALF_P, fb_s.at[j], fb_r.at[j], y_dev(-1))

    def y_far(k):
        for j, zo in offsets(k):
            arrive((zo, 2), 0, HALF_P, ff_s.at[j], ff_r.at[j])
            arrive((zo, 2), HALF_P, HALF_P, fb_s.at[j], fb_r.at[j])

    def message(j, zo, m):
        e, before, second = tab_s[0, j], tab_s[1, j], tab_s[2, j]
        q = at(zo, m)
        block = jnp.where(second == 1, held[q, pl.ds(BLOCK, BLOCK)], held[q, pl.ds(0, BLOCK)])
        product = jnp.dot(values[e], block, preferred_element_type=F32)
        chain[j] = product + chain[before]

    def messages(k):
        for i, zo in offsets(k):
            for m in range(NY):
                message(i * NY + m, zo, m)

    p_step(1)
    send((0, 0), ROWS_P, ROWS_Q, q0_s.at[0], q0_r.at[0], y_dev(1))
    send((0, 0), ROWS_P, ROWS_Q, q0_s.at[1], q0_r.at[1], y_dev(-1))
    send((0, 0), ROWS_P, ROWS_Q, q0_s.at[2], q0_r.at[2], y_dev(2))
    q_step(1, 0)
    y_step(0)

    lanes = lax.broadcasted_iota(I32, (PARTS, PARTS), 1)
    subs = lax.broadcasted_iota(I32, (PARTS, PARTS), 0)

    def as_column(row):
        return jnp.sum(jnp.where(lanes == subs, row, 0), axis=1, keepdims=True)

    def as_row(column):
        return jnp.sum(jnp.where(lanes == subs, column, 0), axis=0, keepdims=True)

    index = subs[:, :1]
    step = index // NY
    z_off = jnp.where(step % 2 == 1, -((step + 1) // 2), step // 2)
    part = ((z + z_off + NZ) % NZ) * NY + (y + index % NY) % NY
    entry = lanes[:1, :]
    slot_of = (table[0] // 2 * REL + table[2]) * 2 + table[0] % 2
    slot_of = jnp.where(entry < count[0], slot_of, SLOTS + entry)
    reads = jnp.where(table[1] == part, 1, 0)
    entry_at = jnp.max(reads * entry, axis=1, keepdims=True)
    slot_at = jnp.max(reads * slot_of, axis=1, keepdims=True)
    pick_at = jnp.sum(jnp.where(entry == part, pick[...], 0), axis=1, keepdims=True)
    slot_row = as_row(slot_at)
    earlier = jnp.max(jnp.where((slot_row == slot_at) & (lanes < subs), lanes, -1), axis=1, keepdims=True)
    earlier = jnp.where(earlier < 0, PARTS, earlier)
    tab[...] = jnp.zeros_like(tab)
    tab[0:1, 0:PARTS] = as_row(entry_at)
    tab[1:2, 0:PARTS] = as_row(earlier)
    tab[2:3, 0:PARTS] = as_row(pick_at)
    slot_lane = lax.broadcasted_iota(I32, (PARTS, BLOCK), 1)
    order = lax.broadcasted_iota(I32, (PARTS, BLOCK), 0)
    final = jnp.max(jnp.where(slot_at == slot_lane, order, -1), axis=0, keepdims=True)
    tab[3:4, :] = jnp.where(final < 0, PARTS, final)
    chain[PARTS] = jnp.zeros((BLOCK, D), F32)

    arrive((0, -1), ROWS_P, ROWS_Q, q0_s.at[0], q0_r.at[0])
    q_step(1, 3)
    arrive((0, 1), ROWS_P, ROWS_Q, q0_s.at[1], q0_r.at[1])
    q_step(1, 1)
    arrive((0, 2), ROWS_P, ROWS_Q, q0_s.at[2], q0_r.at[2])
    q_step(1, 2)
    tab_copy = pltpu.make_async_copy(tab, tab_s, tab_sem)
    tab_copy.start()
    z_rows[...] = jnp.zeros_like(z_rows)

    events = []
    for k in range(FAR + 1):
        if k > 0:
            events.append((TIME_P[k], 0, k, "p"))
            events.append((TIME_Q[k], 2, k, "q"))
        events.append((max(TIME_Y[k], TIME_P[k] + 0.1), 1, k, "y"))
        events.append((max(TIME_Y[k] + 3.0, TIME_Q[k] + 0.1), 3, k, "m"))
    ready = False
    for _, _, k, kind in sorted(events):
        if kind == "p":
            p_arrive(k)
            if k < FAR:
                p_step(k + 1)
            y_step(k)
        elif kind == "y":
            y_forward(k)
        elif kind == "q":
            for m in (0, 3, 1, 2):
                q_arrive(k, m)
                if k < FAR:
                    q_step(k + 1, m)
        else:
            if not ready:
                val_copy.wait()
                tab_copy.wait()
                ready = True
            y_far(k)
            messages(k)

    w_copy.wait()

    def project(c, into):
        def one(r, carry):
            for h in range(2):
                last = tab_s[3, (c * REL + r) * 2 + h]
                terms[c, r, pl.ds(h * BLOCK, BLOCK)] = chain[last].astype(BF16)
            into[...] += jnp.dot(terms[c, r], weight[r], preferred_element_type=F32)
            return carry

        into[...] = jnp.zeros_like(into)
        lax.fori_loop(0, REL, one, 0)

    def blocks(body):
        def one(b, carry):
            body(pl.ds(pl.multiple_of(b * 32, 32), 32))
            return carry

        lax.fori_loop(0, 2 * BLOCK // 32, one, 0)

    panels = [x_at(2), x_at(-turn), x_at(turn), s]
    partner_panels = [x_at(2), x_at(turn), x_at(-turn), s]
    ahead, behind = x_dev(turn), x_dev(-turn)
    swaps, moves = [], []

    def combine(i):
        swaps[i].wait_recv()
        if i == 2:
            moves[0].wait_recv()

        def one(part):
            value = keep[i, part] + ex[i, part].astype(F32)
            if i == 2:
                value = value + cr[0, part].astype(F32)
            cs[i, part] = value.astype(BF16)

        blocks(one)
        moves.append(go(remote(cs.at[i], cr.at[i], cx_s.at[i], cx_r.at[i], behind if i == 1 else ahead)))

    for i in range(4):
        project(partner_panels[i] * 2 + 1 - g, work)

        def narrow(part):
            give[i, part] = work[part].astype(BF16)

        blocks(narrow)
        if i > 0:
            combine(i - 1)
        project(panels[i] * 2 + g, keep.at[i])
        swaps.append(go(remote(give.at[i], ex.at[i], ex_s.at[i], ex_r.at[i], partner)))
    swaps[3].wait_recv()
    moves[1].wait_recv()
    moves[2].wait_recv()
    own = s * 2 + g

    def activate(part):
        value = keep[3, part] + ex[3, part].astype(F32) + cr[1, part].astype(F32) + cr[2, part].astype(F32)
        logistic = 1.0 / (1.0 + jnp.exp(-value))
        result[part] = (value * logistic).astype(BF16)
        slope = logistic * (1.0 + value * (1.0 - logistic))
        rows[own, part] = (cot[part].astype(F32) * slope).astype(BF16)

    blocks(activate)

    def share(c, sem, to):
        return go(remote(rows.at[c], rows.at[c], gx_s.at[sem], gx_r.at[sem], to))

    def relay(c, sem):
        return go(remote(rows.at[c], rows.at[c], gp_s.at[sem], gp_r.at[sem], partner))

    gx0 = share(own, 0, ahead)
    gx1 = share(own, 1, behind)
    gp0 = relay(own, 0)
    out_copy = pltpu.make_async_copy(result, out, out_sem.at[0])
    out_copy.start()

    def add_terms(c, first=False):
        def one(r, carry):
            product = lax.dot_general(terms[c, r], rows[c], (((0,), (0,)), ((), ())),
                                      preferred_element_type=F32)
            if first:
                acc[r] = product
            else:
                acc[r] = acc[r] + product
            return carry

        lax.fori_loop(0, REL, one, 0)

    add_terms(own, first=True)
    gp0.wait_recv()
    add_terms(s * 2 + 1 - g)
    gx0.wait_recv()
    from_behind, from_ahead, from_far = x_at(-turn) * 2 + g, x_at(turn) * 2 + g, x_at(2) * 2 + g
    gx2 = share(from_behind, 2, ahead)
    gp1 = relay(from_behind, 1)
    gx1.wait_recv()
    gp2 = relay(from_ahead, 2)
    add_terms(from_behind)
    add_terms(from_ahead)
    gp1.wait_recv()
    add_terms(x_at(turn) * 2 + 1 - g)
    gp2.wait_recv()
    add_terms(x_at(-turn) * 2 + 1 - g)
    gx2.wait_recv()
    gp3 = relay(from_far, 3)
    add_terms(from_far)
    gp3.wait_recv()
    add_terms(x_at(2) * 2 + 1 - g)

    def ring_sum(load, stage, got, ss, rs, lane, pos, dev):
        copies = {}

        def put(k, p, to, extra):
            for r in range(3):
                value = load(r, p)
                if extra:
                    value = value + got[0, r].astype(F32)
                stage[k, r] = value.astype(BF16)
            copies[k] = go(remote(stage.at[k], got.at[k], ss.at[lane, k], rs.at[lane, k], to))

        def begin():
            put(0, pos(2), dev(turn), False)
            put(1, pos(-turn), dev(-turn), False)

        def middle():
            copies[0].wait_recv()
            put(2, pos(turn), dev(turn), True)

        def end(store):
            copies[1].wait_recv()
            copies[2].wait_recv()
            for r in range(3):
                store(r, load(r, pos(0)) + got[1, r].astype(F32) + got[2, r].astype(F32))

        return begin, middle, end

    def both(one, two, *ends):
        one[0]()
        two[0]()
        one[1]()
        two[1]()
        one[2](*ends[:1])
        two[2](*ends[1:])

    def into_a(r, value):
        a_sum[r] = value

    def into_b(r, value):
        b_sum[r] = value

    def into_tail_a(r, value):
        tail[r] = value

    def into_tail_b(r, value):
        tail[3 + r] = value

    both(ring_sum(lambda r, p: acc[r, pl.ds(p * 64, 64)], a_send, a_recv, s1_s, s1_r, 0, x_at, x_dev),
         ring_sum(lambda r, p: acc[3 + r, pl.ds(p * 64, 64)], b_send, b_recv, s1_s, s1_r, 1, y_at, y_dev),
         into_a, into_b)
    both(ring_sum(lambda r, p: a_sum[r, pl.ds(p * 16, 16)], a2_send, a2_recv, s2_s, s2_r, 0, y_at, y_dev),
         ring_sum(lambda r, p: b_sum[r, pl.ds(p * 16, 16)], b2_send, b2_recv, s2_s, s2_r, 1, x_at, x_dev),
         into_tail_a, into_tail_b)
    for j in range(NZ):
        for r in range(REL):
            for h in range(2):
                z_rows[j, pl.ds(2 * r + h, 1)] = tail[r, pl.ds(j, 1), pl.ds(h * BLOCK, BLOCK)]
    z_send[...] = z_rows[...].astype(BF16)
    third = []
    for d in range(1, NZ):
        to = (z + d) % NZ
        third.append(go(remote(z_send.at[to], z_recv.at[d], z1_s.at[d], z1_r.at[d], z_dev(d))))
    value = z_rows[z]
    for d in range(1, NZ):
        third[d - 1].wait_recv()
        value = value + z_recv[d].astype(F32)
    z_full[z] = value.astype(BF16)

    fourth = []
    for d in range(1, NZ):
        fourth.append(go(remote(z_full.at[z], z_full.at[z], z2_s.at[d], z2_r.at[d], z_dev(d))))
    for copy in fourth:
        copy.wait_recv()
    z_rows[...] = z_full[...].astype(F32)
    for j in range(NZ):
        for r in range(REL):
            for h in range(2):
                tail[r, pl.ds(j, 1), pl.ds(h * BLOCK, BLOCK)] = z_rows[j, pl.ds(2 * r + h, 1)]
    for r in range(3):
        a_all[s, y, r] = tail[r].astype(BF16)
        b_all[y, s, r] = tail[3 + r].astype(BF16)

    def ring_spread(ref, ss, rs, lane, pos, dev):
        copies = {}

        def put(k, p, to):
            copies[k] = go(remote(ref(p), ref(p), ss.at[lane, k], rs.at[lane, k], to))

        def begin():
            put(0, pos(0), dev(turn))
            put(1, pos(0), dev(-turn))

        def middle():
            copies[0].wait_recv()
            put(2, pos(-turn), dev(turn))

        def end():
            copies[1].wait_recv()
            copies[2].wait_recv()

        return begin, middle, end

    both(ring_spread(lambda p: a_all.at[s, p], s4_s, s4_r, 0, y_at, y_dev),
         ring_spread(lambda p: b_all.at[y, p], s4_s, s4_r, 1, x_at, x_dev))
    both(ring_spread(lambda p: a_all.at[p], s5_s, s5_r, 0, x_at, x_dev),
         ring_spread(lambda p: b_all.at[p], s5_s, s5_r, 1, y_at, y_dev))
    a_copy = pltpu.make_async_copy(a_all, a_out, out_sem.at[1])
    b_copy = pltpu.make_async_copy(b_all, b_out, out_sem.at[2])
    a_copy.start()
    b_copy.start()
    for copy in sent:
        copy.wait_send()
    out_copy.wait()
    a_copy.wait()
    b_copy.wait()


def layer(source_feats, table, pick, count, values, weight, cotangent):
    hbm = pl.BlockSpec(memory_space=pl.ANY)
    vmem = pl.BlockSpec(memory_space=pltpu.VMEM)
    smem = pl.BlockSpec(memory_space=pltpu.SMEM)
    dma = pltpu.SemaphoreType.DMA
    V = pltpu.VMEM
    steps = FAR + 1
    slots = values.shape[0]
    sums = jax.ShapeDtypeStruct((4, 4, 3, 16, D), BF16)
    return pl.pallas_call(
        layer_kernel,
        out_shape=(jax.ShapeDtypeStruct((2 * BLOCK, D), BF16), sums, sums),
        in_specs=[hbm, vmem, vmem, smem, hbm, hbm, vmem],
        out_specs=(hbm, hbm, hbm),
        scratch_shapes=[
            V((PARTS, 2 * BLOCK, D), BF16), V((slots, BLOCK, BLOCK), BF16), V((REL, D, D), BF16),
            V((PARTS + 1, BLOCK, D), F32), V((8, BLOCK), I32), pltpu.SMEM((8, BLOCK), I32),
            V((CHUNKS, REL, 256, D), BF16), V((256, D), F32), V((4, 256, D), F32), V((4, 256, D), BF16),
            V((4, 256, D), BF16), V((3, 256, D), BF16), V((3, 256, D), BF16), V((CHUNKS, 256, D), BF16),
            V((REL, D, D), F32),
            V((256, D), BF16), V((4, 4, 3, 16, D), BF16), V((4, 4, 3, 16, D), BF16),
            V((3, 3, 64, D), BF16), V((3, 3, 64, D), BF16), V((3, 3, 64, D), BF16), V((3, 3, 64, D), BF16),
            V((3, 64, D), F32), V((3, 64, D), F32),
            V((3, 3, 16, D), BF16), V((3, 3, 16, D), BF16), V((3, 3, 16, D), BF16), V((3, 3, 16, D), BF16),
            V((REL, 16, D), F32), V((NZ, 16, BLOCK), F32), V((NZ, 16, BLOCK), BF16),
            V((NZ, 16, BLOCK), BF16), V((NZ, 16, BLOCK), BF16),
            dma, dma, dma, dma, dma((3,))]
        + [dma((steps,))] * 4 + [dma((NZ,))] * 8 + [dma((3,))] * 2 + [dma((steps, NY))] * 4
        + [dma((4,))] * 2 + [dma((3,))] * 2 + [dma((3,))] * 2 + [dma((4,))] * 2
        + [dma((2, 3))] * 4 + [dma((NZ,))] * 4 + [dma((2, 3))] * 4,
        compiler_params=pltpu.CompilerParams(
            collective_id=0, has_side_effects=True, vmem_limit_bytes=60 << 20),
        name="layer",
    )(source_feats, table, pick, count, values, weight, cotangent)


def finish_kernel(result, a_all, b_all, out, grad):
    out[...] = result[...]
    for i in range(4):
        for j in range(4):
            part = pl.ds(64 * i + 16 * j, 16)
            for r in range(3):
                grad[r, part] = a_all[i, j, r].astype(F32)
                grad[3 + r, part] = b_all[i, j, r].astype(F32)


def finish(result, a_all, b_all):
    vmem = pl.BlockSpec(memory_space=pltpu.VMEM)
    return pl.pallas_call(
        finish_kernel,
        out_shape=(jax.ShapeDtypeStruct((2 * BLOCK, D), BF16),
                   jax.ShapeDtypeStruct((REL, D, D), F32)),
        in_specs=[vmem] * 3,
        out_specs=(vmem, vmem),
        name="finish",
    )(result, a_all, b_all)


def local(source_feats, rel_weight, halo_pick, entry_index, entry_count, entry_values, cotangent):
    slots = entry_index.shape[-1]
    return finish(*layer(
        source_feats, entry_index.reshape(3, 1, slots), halo_pick.reshape(1, -1), entry_count.reshape(1),
        entry_values.reshape(slots, BLOCK, BLOCK), rel_weight, cotangent))


def solution(mesh):
    return jax.shard_map(
        local,
        mesh=mesh,
        in_specs=(
            P(("dom", "src", "rel"), None),
            P("rel", None, None),
            P("dom", "src", "rel", None),
            P("dom", "src", "rel", None, None),
            P("dom", "src", "rel"),
            P("dom", "src", "rel", None, None, None),
            P(("dom", "src", "rel"), None),
        ),
        out_specs=(P(("dom", "src", "rel"), None), P("rel", None, None)),
        check_vma=False,
    )
```

```python
import jax
import jax.numpy as jnp
from jax import lax
from jax.experimental import pallas as pl
from jax.experimental.pallas import tpu as pltpu
from jax.sharding import PartitionSpec as P

MESH = pl.DeviceIdType.MESH
F32 = jnp.float32
BF16 = jnp.bfloat16
I32 = jnp.int32

NY = 4
NZ = 16
NX = 4
PARTS = 64
BLOCK = 128
D = 256
REL = 6
CHUNKS = 8
SLOTS = CHUNKS * REL * 2
ROWS_P = 96
HALF_P = 48
ROWS_Q = 32
HALF_Q = 16
FAR = NZ // 2

TIME_P = [5.0 * k for k in range(FAR + 1)]
TIME_Q = [5.0 * k + 1.0 for k in range(FAR + 1)]
TIME_Y = [5.0 * k + 6.0 for k in range(FAR + 1)]
MESSAGE_LAG = 8.5


def remote(src, dst, send_sem, recv_sem, to):
    return pltpu.make_async_remote_copy(
        src_ref=src, dst_ref=dst, send_sem=send_sem, recv_sem=recv_sem,
        device_id=to, device_id_type=MESH)


def choose(second, one, zero):
    return jnp.where(second == 1, one, zero)


def offsets(k):
    if k == 0:
        return [(0, 0)]
    if k == FAR:
        return [(2 * k - 1, k)]
    return [(2 * k - 1, -k), (2 * k, k)]


def layer_kernel(src, table, pick, count, values_hbm, weight_hbm, cot,
                 out, a_out, b_out,
                 held, got, stage_up, stage_down, stage_far, relay_up, relay_down, my_pick, peer_pick, peer_s,
                 values, weight, chain, tab, tab_s, terms, work, keep, give, ex, cs, cr, rows, acc,
                 result, a_all, b_all,
                 a_send, a_recv, b_send, b_recv, a_sum, b_sum,
                 a2_send, a2_recv, b2_send, b2_recv, tail, z_rows, z_send, z_recv, z_full,
                 own_sem, val_sem, w_sem, tab_sem, out_sem, pick_sem, pp_s, pp_r, hu_s, hu_r, hd_s, hd_r,
                 pf_s, pf_r, pb_s, pb_r, yf_s, yf_r, yb_s, yb_r,
                 ff_s, ff_r, fb_s, fb_r, q0_s, q0_r, qf_s, qf_r, qb_s, qb_r,
                 ex_s, ex_r, cx_s, cx_r, gx_s, gx_r, gp_s, gp_r,
                 s1_s, s1_r, s2_s, s2_r, z1_s, z1_r, z2_s, z2_r, s4_s, s4_r, s5_s, s5_r):
    dom, s, g = lax.axis_index("dom"), lax.axis_index("src"), lax.axis_index("rel")
    z, y = dom // NY, dom % NY
    turn = 1 - 2 * g
    partner = {"rel": 1 - g}

    def at(zo, yo):
        return ((z + zo + NZ) % NZ) * NY + (y + yo + NY) % NY

    def x_at(o):
        return (s + o + NX) % NX

    def y_at(o):
        return (y + o + NY) % NY

    def x_dev(o):
        return {"src": x_at(o)}

    def y_dev(o):
        return {"dom": z * NY + y_at(o)}

    def z_dev(o):
        return {"dom": ((z + o + NZ) % NZ) * NY + y}

    own_copy = pltpu.make_async_copy(src, held.at[dom], own_sem)
    own_copy.start()
    val_copy = pltpu.make_async_copy(values_hbm, values, val_sem)
    val_copy.start()
    w_copy = pltpu.make_async_copy(weight_hbm, weight, w_sem)
    w_copy.start()

    near = [partner, x_dev(1), x_dev(-1), y_dev(1), y_dev(-1), y_dev(2), z_dev(1), z_dev(-1)]
    barrier = pltpu.get_barrier_semaphore()
    for to in near:
        pl.semaphore_signal(barrier, inc=1, device_id=to, device_id_type=MESH)
    my_pick[...] = jnp.zeros_like(my_pick)
    my_pick[0:1, 0:PARTS] = pick[...]
    own_copy.wait()
    pl.semaphore_wait(barrier, len(near))

    sent = []

    def go(copy):
        copy.start()
        sent.append(copy)
        return copy

    def send(where, row, n, s_sem, r_sem, to):
        ref = held.at[at(*where), :, pl.ds(row, n)]
        go(remote(ref, ref, s_sem, r_sem, to))

    def arrive(where, row, n, s_sem, r_sem):
        ref = held.at[at(*where), :, pl.ds(row, n)]
        remote(ref, ref, s_sem, r_sem, z_dev(1)).wait_recv()

    def cut(k, low, full, half, back):
        if k < FAR:
            return low, full
        return low + (half if back else 0), half

    def p_step(k):
        send((-(k - 1), 0), *cut(k, 0, ROWS_P, HALF_P, False), pf_s.at[k], pf_r.at[k], z_dev(1))
        send((k - 1, 0), *cut(k, 0, ROWS_P, HALF_P, True), pb_s.at[k], pb_r.at[k], z_dev(-1))

    def p_arrive(k):
        arrive((-k, 0), *cut(k, 0, ROWS_P, HALF_P, False), pf_s.at[k], pf_r.at[k])
        arrive((k, 0), *cut(k, 0, ROWS_P, HALF_P, True), pb_s.at[k], pb_r.at[k])

    def q_step(k, m):
        send((-(k - 1), m), *cut(k, ROWS_P, ROWS_Q, HALF_Q, False), qf_s.at[k, m], qf_r.at[k, m], z_dev(1))
        send((k - 1, m), *cut(k, ROWS_P, ROWS_Q, HALF_Q, True), qb_s.at[k, m], qb_r.at[k, m], z_dev(-1))

    def q_arrive(k, m):
        arrive((-k, m), *cut(k, ROWS_P, ROWS_Q, HALF_Q, False), qf_s.at[k, m], qf_r.at[k, m])
        arrive((k, m), *cut(k, ROWS_P, ROWS_Q, HALF_Q, True), qb_s.at[k, m], qb_r.at[k, m])

    def y_step(k):
        for j, zo in offsets(k):
            q = at(zo, 0)
            top = pl.ds(0, ROWS_P)
            stage_far[j] = choose(peer_s[2, 0, q], held[q, 1, top], held[q, 0, top])
            stage_up[j] = choose(peer_s[0, 0, q], held[q, 1, top], held[q, 0, top])
            stage_down[j] = choose(peer_s[1, 0, q], held[q, 1, top], held[q, 0, top])
            go(remote(stage_far.at[j, pl.ds(0, HALF_P)], relay_up.at[j], hu_s.at[j], hu_r.at[j], y_dev(1)))
            go(remote(stage_far.at[j, pl.ds(HALF_P, HALF_P)], relay_down.at[j], hd_s.at[j], hd_r.at[j], y_dev(-1)))
            go(remote(stage_up.at[j], got.at[j, 3, top], yf_s.at[j], yf_r.at[j], y_dev(1)))
            go(remote(stage_down.at[j], got.at[j, 1, top], yb_s.at[j], yb_r.at[j], y_dev(-1)))

    def landed(ref, s_sem, r_sem):
        remote(ref, ref, s_sem, r_sem, y_dev(1)).wait_recv()

    def y_forward(k):
        for j, zo in offsets(k):
            landed(relay_up.at[j], hu_s.at[j], hu_r.at[j])
            go(remote(relay_up.at[j], got.at[j, 2, pl.ds(0, HALF_P)], ff_s.at[j], ff_r.at[j], y_dev(1)))
            landed(relay_down.at[j], hd_s.at[j], hd_r.at[j])
            go(remote(relay_down.at[j], got.at[j, 2, pl.ds(HALF_P, HALF_P)], fb_s.at[j], fb_r.at[j], y_dev(-1)))

    def y_far(k):
        for j, zo in offsets(k):
            landed(got.at[j, 3, pl.ds(0, ROWS_P)], yf_s.at[j], yf_r.at[j])
            landed(got.at[j, 1, pl.ds(0, ROWS_P)], yb_s.at[j], yb_r.at[j])
            landed(got.at[j, 2, pl.ds(0, HALF_P)], ff_s.at[j], ff_r.at[j])
            landed(got.at[j, 2, pl.ds(HALF_P, HALF_P)], fb_s.at[j], fb_r.at[j])

    def message(i, zo, m):
        j = i * NY + m
        e, before, second = tab_s[0, j], tab_s[1, j], tab_s[2, j]
        q = at(zo, m)
        if m == 0:
            block = choose(second, held[q, 1], held[q, 0])
        else:
            rest = pl.ds(ROWS_P, ROWS_Q)
            block = jnp.concatenate(
                [got[i, m, pl.ds(0, ROWS_P)], choose(second, held[q, 1, rest], held[q, 0, rest])], axis=0)
        product = jnp.dot(values[e], block, preferred_element_type=F32)
        chain[j] = product + chain[before]

    def messages(k):
        for i, zo in offsets(k):
            for m in range(NY):
                message(i, zo, m)

    p_step(1)
    swaps_of_picks = []
    for i, o in enumerate((1, -1, 2)):
        there = (1, 0, 2)[i]
        swaps_of_picks.append(go(remote(my_pick, peer_pick.at[there], pp_s.at[i], pp_r.at[there], y_dev(o))))
    send((0, 0), ROWS_P, ROWS_Q, q0_s.at[0], q0_r.at[0], y_dev(1))
    send((0, 0), ROWS_P, ROWS_Q, q0_s.at[1], q0_r.at[1], y_dev(-1))
    send((0, 0), ROWS_P, ROWS_Q, q0_s.at[2], q0_r.at[2], y_dev(2))
    q_step(1, 0)

    for i in range(3):
        landed(peer_pick.at[i], pp_s.at[i], pp_r.at[i])
    pick_copy = pltpu.make_async_copy(peer_pick, peer_s, pick_sem)
    pick_copy.start()
    pick_copy.wait()
    y_step(0)

    lanes = lax.broadcasted_iota(I32, (PARTS, PARTS), 1)
    subs = lax.broadcasted_iota(I32, (PARTS, PARTS), 0)

    def as_column(row):
        return jnp.sum(jnp.where(lanes == subs, row, 0), axis=1, keepdims=True)

    def as_row(column):
        return jnp.sum(jnp.where(lanes == subs, column, 0), axis=0, keepdims=True)

    index = subs[:, :1]
    step = index // NY
    z_off = jnp.where(step % 2 == 1, -((step + 1) // 2), step // 2)
    part = ((z + z_off + NZ) % NZ) * NY + (y + index % NY) % NY
    entry = lanes[:1, :]
    slot_of = (table[0] // 2 * REL + table[2]) * 2 + table[0] % 2
    slot_of = jnp.where(entry < count[0], slot_of, SLOTS + entry)
    reads = jnp.where(table[1] == part, 1, 0)
    entry_at = jnp.max(reads * entry, axis=1, keepdims=True)
    slot_at = jnp.max(reads * slot_of, axis=1, keepdims=True)
    pick_at = jnp.sum(jnp.where(entry == part, pick[...], 0), axis=1, keepdims=True)
    slot_row = as_row(slot_at)
    earlier = jnp.max(jnp.where((slot_row == slot_at) & (lanes < subs), lanes, -1), axis=1, keepdims=True)
    earlier = jnp.where(earlier < 0, PARTS, earlier)
    tab[...] = jnp.zeros_like(tab)
    tab[0:1, 0:PARTS] = as_row(entry_at)
    tab[1:2, 0:PARTS] = as_row(earlier)
    tab[2:3, 0:PARTS] = as_row(pick_at)
    slot_lane = lax.broadcasted_iota(I32, (PARTS, BLOCK), 1)
    order = lax.broadcasted_iota(I32, (PARTS, BLOCK), 0)
    final = jnp.max(jnp.where(slot_at == slot_lane, order, -1), axis=0, keepdims=True)
    tab[3:4, :] = jnp.where(final < 0, PARTS, final)
    chain[PARTS] = jnp.zeros((BLOCK, D), F32)

    arrive((0, -1), ROWS_P, ROWS_Q, q0_s.at[0], q0_r.at[0])
    q_step(1, 3)
    arrive((0, 1), ROWS_P, ROWS_Q, q0_s.at[1], q0_r.at[1])
    q_step(1, 1)
    arrive((0, 2), ROWS_P, ROWS_Q, q0_s.at[2], q0_r.at[2])
    q_step(1, 2)
    tab_copy = pltpu.make_async_copy(tab, tab_s, tab_sem)
    tab_copy.start()
    z_rows[...] = jnp.zeros_like(z_rows)

    events = []
    for k in range(FAR + 1):
        if k > 0:
            events.append((TIME_P[k], 0, k, "p"))
            events.append((TIME_Q[k], 2, k, "q"))
        events.append((max(TIME_Y[k], TIME_P[k] + 0.1), 1, k, "y"))
        events.append((max(TIME_Y[k] + MESSAGE_LAG, TIME_Q[k] + 0.1), 3, k, "m"))
    ready = False
    for _, _, k, kind in sorted(events):
        if kind == "p":
            p_arrive(k)
            if k < FAR:
                p_step(k + 1)
            y_step(k)
        elif kind == "y":
            y_forward(k)
        elif kind == "q":
            for m in (0, 3, 1, 2):
                q_arrive(k, m)
                if k < FAR:
                    q_step(k + 1, m)
        else:
            if not ready:
                val_copy.wait()
                tab_copy.wait()
                ready = True
            y_far(k)
            messages(k)

    w_copy.wait()

    def project(c, into):
        def one(r, carry):
            for h in range(2):
                last = tab_s[3, (c * REL + r) * 2 + h]
                terms[c, r, pl.ds(h * BLOCK, BLOCK)] = chain[last].astype(BF16)
            into[...] += jnp.dot(terms[c, r], weight[r], preferred_element_type=F32)
            return carry

        into[...] = jnp.zeros_like(into)
        lax.fori_loop(0, REL, one, 0)

    def blocks(body):
        def one(b, carry):
            body(pl.ds(pl.multiple_of(b * 32, 32), 32))
            return carry

        lax.fori_loop(0, 2 * BLOCK // 32, one, 0)

    panels = [x_at(2), x_at(-turn), x_at(turn), s]
    partner_panels = [x_at(2), x_at(turn), x_at(-turn), s]
    ahead, behind = x_dev(turn), x_dev(-turn)
    swaps, moves = [], []

    def combine(i):
        swaps[i].wait_recv()
        if i == 2:
            moves[0].wait_recv()

        def one(part):
            value = keep[i, part] + ex[i, part].astype(F32)
            if i == 2:
                value = value + cr[0, part].astype(F32)
            cs[i, part] = value.astype(BF16)

        blocks(one)
        moves.append(go(remote(cs.at[i], cr.at[i], cx_s.at[i], cx_r.at[i], behind if i == 1 else ahead)))

    for i in range(4):
        project(partner_panels[i] * 2 + 1 - g, work)

        def narrow(part):
            give[i, part] = work[part].astype(BF16)

        blocks(narrow)
        if i > 0:
            combine(i - 1)
        project(panels[i] * 2 + g, keep.at[i])
        swaps.append(go(remote(give.at[i], ex.at[i], ex_s.at[i], ex_r.at[i], partner)))
    swaps[3].wait_recv()
    moves[1].wait_recv()
    moves[2].wait_recv()
    own = s * 2 + g

    def activate(part):
        value = keep[3, part] + ex[3, part].astype(F32) + cr[1, part].astype(F32) + cr[2, part].astype(F32)
        logistic = 1.0 / (1.0 + jnp.exp(-value))
        result[part] = (value * logistic).astype(BF16)
        slope = logistic * (1.0 + value * (1.0 - logistic))
        rows[own, part] = (cot[part].astype(F32) * slope).astype(BF16)

    blocks(activate)

    def share(c, sem, to):
        return go(remote(rows.at[c], rows.at[c], gx_s.at[sem], gx_r.at[sem], to))

    def relay(c, sem):
        return go(remote(rows.at[c], rows.at[c], gp_s.at[sem], gp_r.at[sem], partner))

    gx0 = share(own, 0, ahead)
    gx1 = share(own, 1, behind)
    gp0 = relay(own, 0)
    out_copy = pltpu.make_async_copy(result, out, out_sem.at[0])
    out_copy.start()

    def add_terms(c, first=False):
        def one(r, carry):
            product = lax.dot_general(terms[c, r], rows[c], (((0,), (0,)), ((), ())),
                                      preferred_element_type=F32)
            if first:
                acc[r] = product
            else:
                acc[r] = acc[r] + product
            return carry

        lax.fori_loop(0, REL, one, 0)

    add_terms(own, first=True)
    gp0.wait_recv()
    add_terms(s * 2 + 1 - g)
    gx0.wait_recv()
    from_behind, from_ahead, from_far = x_at(-turn) * 2 + g, x_at(turn) * 2 + g, x_at(2) * 2 + g
    gx2 = share(from_behind, 2, ahead)
    gp1 = relay(from_behind, 1)
    gx1.wait_recv()
    gp2 = relay(from_ahead, 2)
    add_terms(from_behind)
    add_terms(from_ahead)
    gp1.wait_recv()
    add_terms(x_at(turn) * 2 + 1 - g)
    gp2.wait_recv()
    add_terms(x_at(-turn) * 2 + 1 - g)
    gx2.wait_recv()
    gp3 = relay(from_far, 3)
    add_terms(from_far)
    gp3.wait_recv()
    add_terms(x_at(2) * 2 + 1 - g)

    def ring_sum(load, stage, got, ss, rs, lane, pos, dev):
        copies = {}

        def put(k, p, to, extra):
            for r in range(3):
                value = load(r, p)
                if extra:
                    value = value + got[0, r].astype(F32)
                stage[k, r] = value.astype(BF16)
            copies[k] = go(remote(stage.at[k], got.at[k], ss.at[lane, k], rs.at[lane, k], to))

        def begin():
            put(0, pos(2), dev(turn), False)
            put(1, pos(-turn), dev(-turn), False)

        def middle():
            copies[0].wait_recv()
            put(2, pos(turn), dev(turn), True)

        def end(store):
            copies[1].wait_recv()
            copies[2].wait_recv()
            for r in range(3):
                store(r, load(r, pos(0)) + got[1, r].astype(F32) + got[2, r].astype(F32))

        return begin, middle, end

    def both(one, two, *ends):
        one[0]()
        two[0]()
        one[1]()
        two[1]()
        one[2](*ends[:1])
        two[2](*ends[1:])

    def into_a(r, value):
        a_sum[r] = value

    def into_b(r, value):
        b_sum[r] = value

    def into_tail_a(r, value):
        tail[r] = value

    def into_tail_b(r, value):
        tail[3 + r] = value

    both(ring_sum(lambda r, p: acc[r, pl.ds(p * 64, 64)], a_send, a_recv, s1_s, s1_r, 0, x_at, x_dev),
         ring_sum(lambda r, p: acc[3 + r, pl.ds(p * 64, 64)], b_send, b_recv, s1_s, s1_r, 1, y_at, y_dev),
         into_a, into_b)
    both(ring_sum(lambda r, p: a_sum[r, pl.ds(p * 16, 16)], a2_send, a2_recv, s2_s, s2_r, 0, y_at, y_dev),
         ring_sum(lambda r, p: b_sum[r, pl.ds(p * 16, 16)], b2_send, b2_recv, s2_s, s2_r, 1, x_at, x_dev),
         into_tail_a, into_tail_b)
    for j in range(NZ):
        for r in range(REL):
            for h in range(2):
                z_rows[j, pl.ds(2 * r + h, 1)] = tail[r, pl.ds(j, 1), pl.ds(h * BLOCK, BLOCK)]
    z_send[...] = z_rows[...].astype(BF16)
    third = []
    for d in range(1, NZ):
        to = (z + d) % NZ
        third.append(go(remote(z_send.at[to], z_recv.at[d], z1_s.at[d], z1_r.at[d], z_dev(d))))
    value = z_rows[z]
    for d in range(1, NZ):
        third[d - 1].wait_recv()
        value = value + z_recv[d].astype(F32)
    z_full[z] = value.astype(BF16)

    fourth = []
    for d in range(1, NZ):
        fourth.append(go(remote(z_full.at[z], z_full.at[z], z2_s.at[d], z2_r.at[d], z_dev(d))))
    for copy in fourth:
        copy.wait_recv()
    z_rows[...] = z_full[...].astype(F32)
    for j in range(NZ):
        for r in range(REL):
            for h in range(2):
                tail[r, pl.ds(j, 1), pl.ds(h * BLOCK, BLOCK)] = z_rows[j, pl.ds(2 * r + h, 1)]
    for r in range(3):
        a_all[s, y, r] = tail[r].astype(BF16)
        b_all[y, s, r] = tail[3 + r].astype(BF16)

    def ring_spread(ref, ss, rs, lane, pos, dev):
        copies = {}

        def put(k, p, to):
            copies[k] = go(remote(ref(p), ref(p), ss.at[lane, k], rs.at[lane, k], to))

        def begin():
            put(0, pos(0), dev(turn))
            put(1, pos(0), dev(-turn))

        def middle():
            copies[0].wait_recv()
            put(2, pos(-turn), dev(turn))

        def end():
            copies[1].wait_recv()
            copies[2].wait_recv()

        return begin, middle, end

    both(ring_spread(lambda p: a_all.at[s, p], s4_s, s4_r, 0, y_at, y_dev),
         ring_spread(lambda p: b_all.at[y, p], s4_s, s4_r, 1, x_at, x_dev))
    both(ring_spread(lambda p: a_all.at[p], s5_s, s5_r, 0, x_at, x_dev),
         ring_spread(lambda p: b_all.at[p], s5_s, s5_r, 1, y_at, y_dev))
    a_copy = pltpu.make_async_copy(a_all, a_out, out_sem.at[1])
    b_copy = pltpu.make_async_copy(b_all, b_out, out_sem.at[2])
    a_copy.start()
    b_copy.start()
    for copy in sent:
        copy.wait_send()
    out_copy.wait()
    a_copy.wait()
    b_copy.wait()


def layer(source_feats, table, pick, count, values, weight, cotangent):
    hbm = pl.BlockSpec(memory_space=pl.ANY)
    vmem = pl.BlockSpec(memory_space=pltpu.VMEM)
    smem = pl.BlockSpec(memory_space=pltpu.SMEM)
    dma = pltpu.SemaphoreType.DMA
    V = pltpu.VMEM
    steps = FAR + 1
    slots = values.shape[0]
    sums = jax.ShapeDtypeStruct((4, 4, 3, 16, D), BF16)
    return pl.pallas_call(
        layer_kernel,
        out_shape=(jax.ShapeDtypeStruct((2 * BLOCK, D), BF16), sums, sums),
        in_specs=[hbm, vmem, vmem, smem, hbm, hbm, vmem],
        out_specs=(hbm, hbm, hbm),
        scratch_shapes=[
            V((PARTS, 2, BLOCK, D), BF16), V((NZ, NY, BLOCK, D), BF16),
            V((NZ, ROWS_P, D), BF16), V((NZ, ROWS_P, D), BF16), V((NZ, ROWS_P, D), BF16),
            V((NZ, HALF_P, D), BF16), V((NZ, HALF_P, D), BF16),
            V((8, BLOCK), I32), V((3, 8, BLOCK), I32), pltpu.SMEM((3, 8, BLOCK), I32),
            V((slots, BLOCK, BLOCK), BF16), V((REL, D, D), BF16),
            V((PARTS + 1, BLOCK, D), F32), V((8, BLOCK), I32), pltpu.SMEM((8, BLOCK), I32),
            V((CHUNKS, REL, 256, D), BF16), V((256, D), F32), V((4, 256, D), F32), V((4, 256, D), BF16),
            V((4, 256, D), BF16), V((3, 256, D), BF16), V((3, 256, D), BF16), V((CHUNKS, 256, D), BF16),
            V((REL, D, D), F32),
            V((256, D), BF16), V((4, 4, 3, 16, D), BF16), V((4, 4, 3, 16, D), BF16),
            V((3, 3, 64, D), BF16), V((3, 3, 64, D), BF16), V((3, 3, 64, D), BF16), V((3, 3, 64, D), BF16),
            V((3, 64, D), F32), V((3, 64, D), F32),
            V((3, 3, 16, D), BF16), V((3, 3, 16, D), BF16), V((3, 3, 16, D), BF16), V((3, 3, 16, D), BF16),
            V((REL, 16, D), F32), V((NZ, 16, BLOCK), F32), V((NZ, 16, BLOCK), BF16),
            V((NZ, 16, BLOCK), BF16), V((NZ, 16, BLOCK), BF16),
            dma, dma, dma, dma, dma((3,)), dma, dma((3,)), dma((3,))]
        + [dma((NZ,))] * 4
        + [dma((steps,))] * 4 + [dma((NZ,))] * 8 + [dma((3,))] * 2 + [dma((steps, NY))] * 4
        + [dma((4,))] * 2 + [dma((3,))] * 2 + [dma((3,))] * 2 + [dma((4,))] * 2
        + [dma((2, 3))] * 4 + [dma((NZ,))] * 4 + [dma((2, 3))] * 4,
        compiler_params=pltpu.CompilerParams(
            collective_id=0, has_side_effects=True, vmem_limit_bytes=60 << 20),
        name="layer",
    )(source_feats, table, pick, count, values, weight, cotangent)


def finish_kernel(result, a_all, b_all, out, grad):
    out[...] = result[...]
    for i in range(4):
        for j in range(4):
            part = pl.ds(64 * i + 16 * j, 16)
            for r in range(3):
                grad[r, part] = a_all[i, j, r].astype(F32)
                grad[3 + r, part] = b_all[i, j, r].astype(F32)


def finish(result, a_all, b_all):
    vmem = pl.BlockSpec(memory_space=pltpu.VMEM)
    return pl.pallas_call(
        finish_kernel,
        out_shape=(jax.ShapeDtypeStruct((2 * BLOCK, D), BF16),
                   jax.ShapeDtypeStruct((REL, D, D), F32)),
        in_specs=[vmem] * 3,
        out_specs=(vmem, vmem),
        name="finish",
    )(result, a_all, b_all)


def local(source_feats, rel_weight, halo_pick, entry_index, entry_count, entry_values, cotangent):
    slots = entry_index.shape[-1]
    return finish(*layer(
        source_feats.reshape(2, BLOCK, D), entry_index.reshape(3, 1, slots), halo_pick.reshape(1, -1), entry_count.reshape(1),
        entry_values.reshape(slots, BLOCK, BLOCK), rel_weight, cotangent))


def solution(mesh):
    return jax.shard_map(
        local,
        mesh=mesh,
        in_specs=(
            P(("dom", "src", "rel"), None),
            P("rel", None, None),
            P("dom", "src", "rel", None),
            P("dom", "src", "rel", None, None),
            P("dom", "src", "rel"),
            P("dom", "src", "rel", None, None, None),
            P(("dom", "src", "rel"), None),
        ),
        out_specs=(P(("dom", "src", "rel"), None), P("rel", None, None)),
        check_vma=False,
    )
```

```python
import jax
import jax.numpy as jnp
from jax import lax
from jax.experimental import pallas as pl
from jax.experimental.pallas import tpu as pltpu
from jax.sharding import PartitionSpec as P

MESH = pl.DeviceIdType.MESH
F32 = jnp.float32
BF16 = jnp.bfloat16
I32 = jnp.int32

NY = 4
NZ = 16
NX = 4
PARTS = 64
BLOCK = 128
D = 256
REL = 6
CHUNKS = 8
SLOTS = CHUNKS * REL * 2
ROWS_P = 96
HALF_P = 48
ROWS_Q = 32
HALF_Q = 16
FAR = NZ // 2

TIME_P = [5.0 * k for k in range(FAR + 1)]
TIME_Q = [5.0 * k + 1.0 for k in range(FAR + 1)]
TIME_Y = [5.0 * k + 6.0 for k in range(FAR + 1)]
MESSAGE_LAG = 8.5


def remote(src, dst, send_sem, recv_sem, to):
    return pltpu.make_async_remote_copy(
        src_ref=src, dst_ref=dst, send_sem=send_sem, recv_sem=recv_sem,
        device_id=to, device_id_type=MESH)


def choose(second, one, zero):
    return jnp.where(second == 1, one, zero)


def offsets(k):
    if k == 0:
        return [(0, 0)]
    if k == FAR:
        return [(2 * k - 1, k)]
    return [(2 * k - 1, -k), (2 * k, k)]


def layer_kernel(src, table, pick, count, values_hbm, weight_hbm, cot,
                 out, a_out, b_out,
                 held, got, stage_up, stage_down, stage_far, relay_up, relay_down, my_pick, peer_pick, peer_s,
                 values, weight, chain, tab, tab_s, terms, work, keep, give, ex, cs, cr, rows, acc,
                 result, a_all, b_all,
                 a_send, a_recv, b_send, b_recv, a_sum, b_sum,
                 a2_send, a2_recv, b2_send, b2_recv, tail, z_rows, z_send, z_recv, z_full,
                 own_sem, val_sem, w_sem, tab_sem, out_sem, pick_sem, pp_s, pp_r, hu_s, hu_r, hd_s, hd_r,
                 pf_s, pf_r, pb_s, pb_r, yf_s, yf_r, yb_s, yb_r,
                 ff_s, ff_r, fb_s, fb_r, q0_s, q0_r, qf_s, qf_r, qb_s, qb_r,
                 ex_s, ex_r, cx_s, cx_r, gx_s, gx_r, gp_s, gp_r,
                 s1_s, s1_r, s2_s, s2_r, z1_s, z1_r, z2_s, z2_r, s4_s, s4_r, s5_s, s5_r):
    dom, s, g = lax.axis_index("dom"), lax.axis_index("src"), lax.axis_index("rel")
    z, y = dom // NY, dom % NY
    turn = 1 - 2 * g
    partner = {"rel": 1 - g}

    def at(zo, yo):
        return ((z + zo + NZ) % NZ) * NY + (y + yo + NY) % NY

    def x_at(o):
        return (s + o + NX) % NX

    def y_at(o):
        return (y + o + NY) % NY

    def x_dev(o):
        return {"src": x_at(o)}

    def y_dev(o):
        return {"dom": z * NY + y_at(o)}

    def z_dev(o):
        return {"dom": ((z + o + NZ) % NZ) * NY + y}

    own_copy = pltpu.make_async_copy(src, held.at[dom], own_sem)
    own_copy.start()
    val_copy = pltpu.make_async_copy(values_hbm, values, val_sem)
    val_copy.start()
    w_copy = pltpu.make_async_copy(weight_hbm, weight, w_sem)
    w_copy.start()

    near = [partner, x_dev(1), x_dev(-1), y_dev(1), y_dev(-1), y_dev(2), z_dev(1), z_dev(-1)]
    barrier = pltpu.get_barrier_semaphore()
    for to in near:
        pl.semaphore_signal(barrier, inc=1, device_id=to, device_id_type=MESH)
    my_pick[...] = jnp.zeros_like(my_pick)
    my_pick[0:1, 0:PARTS] = pick[...]
    own_copy.wait()
    pl.semaphore_wait(barrier, len(near))

    sent = []

    def go(copy):
        copy.start()
        sent.append(copy)
        return copy

    def send(where, row, n, s_sem, r_sem, to):
        ref = held.at[at(*where), :, pl.ds(row, n)]
        go(remote(ref, ref, s_sem, r_sem, to))

    def arrive(where, row, n, s_sem, r_sem):
        ref = held.at[at(*where), :, pl.ds(row, n)]
        remote(ref, ref, s_sem, r_sem, z_dev(1)).wait_recv()

    def cut(k, low, full, half, back):
        if k < FAR:
            return low, full
        return low + (half if back else 0), half

    def p_step(k):
        send((-(k - 1), 0), *cut(k, 0, ROWS_P, HALF_P, False), pf_s.at[k], pf_r.at[k], z_dev(1))
        send((k - 1, 0), *cut(k, 0, ROWS_P, HALF_P, True), pb_s.at[k], pb_r.at[k], z_dev(-1))

    def p_arrive(k):
        arrive((-k, 0), *cut(k, 0, ROWS_P, HALF_P, False), pf_s.at[k], pf_r.at[k])
        arrive((k, 0), *cut(k, 0, ROWS_P, HALF_P, True), pb_s.at[k], pb_r.at[k])

    def q_step(k, m):
        send((-(k - 1), m), *cut(k, ROWS_P, ROWS_Q, HALF_Q, False), qf_s.at[k, m], qf_r.at[k, m], z_dev(1))
        send((k - 1, m), *cut(k, ROWS_P, ROWS_Q, HALF_Q, True), qb_s.at[k, m], qb_r.at[k, m], z_dev(-1))

    def q_arrive(k, m):
        arrive((-k, m), *cut(k, ROWS_P, ROWS_Q, HALF_Q, False), qf_s.at[k, m], qf_r.at[k, m])
        arrive((k, m), *cut(k, ROWS_P, ROWS_Q, HALF_Q, True), qb_s.at[k, m], qb_r.at[k, m])

    def y_step(k):
        for j, zo in offsets(k):
            q = at(zo, 0)
            top = pl.ds(0, ROWS_P)
            stage_far[j] = choose(peer_s[2, 0, q], held[q, 1, top], held[q, 0, top])
            stage_up[j] = choose(peer_s[0, 0, q], held[q, 1, top], held[q, 0, top])
            stage_down[j] = choose(peer_s[1, 0, q], held[q, 1, top], held[q, 0, top])
            go(remote(stage_far.at[j, pl.ds(0, HALF_P)], relay_up.at[j], hu_s.at[j], hu_r.at[j], y_dev(1)))
            go(remote(stage_far.at[j, pl.ds(HALF_P, HALF_P)], relay_down.at[j], hd_s.at[j], hd_r.at[j], y_dev(-1)))
            go(remote(stage_up.at[j], got.at[j, 3, top], yf_s.at[j], yf_r.at[j], y_dev(1)))
            go(remote(stage_down.at[j], got.at[j, 1, top], yb_s.at[j], yb_r.at[j], y_dev(-1)))

    def landed(ref, s_sem, r_sem):
        remote(ref, ref, s_sem, r_sem, y_dev(1)).wait_recv()

    def y_forward(k):
        for j, zo in offsets(k):
            landed(relay_up.at[j], hu_s.at[j], hu_r.at[j])
            go(remote(relay_up.at[j], got.at[j, 2, pl.ds(0, HALF_P)], ff_s.at[j], ff_r.at[j], y_dev(1)))
            landed(relay_down.at[j], hd_s.at[j], hd_r.at[j])
            go(remote(relay_down.at[j], got.at[j, 2, pl.ds(HALF_P, HALF_P)], fb_s.at[j], fb_r.at[j], y_dev(-1)))

    def y_far(k):
        for j, zo in offsets(k):
            landed(got.at[j, 3, pl.ds(0, ROWS_P)], yf_s.at[j], yf_r.at[j])
            landed(got.at[j, 1, pl.ds(0, ROWS_P)], yb_s.at[j], yb_r.at[j])
            landed(got.at[j, 2, pl.ds(0, HALF_P)], ff_s.at[j], ff_r.at[j])
            landed(got.at[j, 2, pl.ds(HALF_P, HALF_P)], fb_s.at[j], fb_r.at[j])

    def message(i, zo, m):
        j = i * NY + m
        e, before, second = tab_s[0, j], tab_s[1, j], tab_s[2, j]
        q = at(zo, m)
        if m == 0:
            block = choose(second, held[q, 1], held[q, 0])
        else:
            rest = pl.ds(ROWS_P, ROWS_Q)
            block = jnp.concatenate(
                [got[i, m, pl.ds(0, ROWS_P)], choose(second, held[q, 1, rest], held[q, 0, rest])], axis=0)
        product = jnp.dot(values[e], block, preferred_element_type=F32)
        chain[j] = product + chain[before]

    def messages(k):
        for i, zo in offsets(k):
            for m in range(NY):
                message(i, zo, m)

    p_step(1)
    swaps_of_picks = []
    for i, o in enumerate((1, -1, 2)):
        there = (1, 0, 2)[i]
        swaps_of_picks.append(go(remote(my_pick, peer_pick.at[there], pp_s.at[i], pp_r.at[there], y_dev(o))))
    send((0, 0), ROWS_P, ROWS_Q, q0_s.at[0], q0_r.at[0], y_dev(1))
    send((0, 0), ROWS_P, ROWS_Q, q0_s.at[1], q0_r.at[1], y_dev(-1))
    send((0, 0), ROWS_P, ROWS_Q, q0_s.at[2], q0_r.at[2], y_dev(2))
    q_step(1, 0)

    for i in range(3):
        landed(peer_pick.at[i], pp_s.at[i], pp_r.at[i])
    pick_copy = pltpu.make_async_copy(peer_pick, peer_s, pick_sem)
    pick_copy.start()
    pick_copy.wait()
    y_step(0)

    lanes = lax.broadcasted_iota(I32, (PARTS, PARTS), 1)
    subs = lax.broadcasted_iota(I32, (PARTS, PARTS), 0)

    def as_column(row):
        return jnp.sum(jnp.where(lanes == subs, row, 0), axis=1, keepdims=True)

    def as_row(column):
        return jnp.sum(jnp.where(lanes == subs, column, 0), axis=0, keepdims=True)

    index = subs[:, :1]
    step = index // NY
    z_off = jnp.where(step % 2 == 1, -((step + 1) // 2), step // 2)
    part = ((z + z_off + NZ) % NZ) * NY + (y + index % NY) % NY
    entry = lanes[:1, :]
    slot_of = (table[0] // 2 * REL + table[2]) * 2 + table[0] % 2
    slot_of = jnp.where(entry < count[0], slot_of, SLOTS + entry)
    reads = jnp.where(table[1] == part, 1, 0)
    entry_at = jnp.max(reads * entry, axis=1, keepdims=True)
    slot_at = jnp.max(reads * slot_of, axis=1, keepdims=True)
    pick_at = jnp.sum(jnp.where(entry == part, pick[...], 0), axis=1, keepdims=True)
    slot_row = as_row(slot_at)
    earlier = jnp.max(jnp.where((slot_row == slot_at) & (lanes < subs), lanes, -1), axis=1, keepdims=True)
    earlier = jnp.where(earlier < 0, PARTS, earlier)
    tab[...] = jnp.zeros_like(tab)
    tab[0:1, 0:PARTS] = as_row(entry_at)
    tab[1:2, 0:PARTS] = as_row(earlier)
    tab[2:3, 0:PARTS] = as_row(pick_at)
    slot_lane = lax.broadcasted_iota(I32, (PARTS, BLOCK), 1)
    order = lax.broadcasted_iota(I32, (PARTS, BLOCK), 0)
    final = jnp.max(jnp.where(slot_at == slot_lane, order, -1), axis=0, keepdims=True)
    tab[3:4, :] = jnp.where(final < 0, PARTS, final)
    chain[PARTS] = jnp.zeros((BLOCK, D), F32)

    arrive((0, -1), ROWS_P, ROWS_Q, q0_s.at[0], q0_r.at[0])
    q_step(1, 3)
    arrive((0, 1), ROWS_P, ROWS_Q, q0_s.at[1], q0_r.at[1])
    q_step(1, 1)
    arrive((0, 2), ROWS_P, ROWS_Q, q0_s.at[2], q0_r.at[2])
    q_step(1, 2)
    tab_copy = pltpu.make_async_copy(tab, tab_s, tab_sem)
    tab_copy.start()
    z_rows[...] = jnp.zeros_like(z_rows)

    events = []
    for k in range(FAR + 1):
        if k > 0:
            events.append((TIME_P[k], 0, k, "p"))
            events.append((TIME_Q[k], 2, k, "q"))
        events.append((max(TIME_Y[k], TIME_P[k] + 0.1), 1, k, "y"))
        events.append((max(TIME_Y[k] + MESSAGE_LAG, TIME_Q[k] + 0.1), 3, k, "m"))
    ready = False
    for _, _, k, kind in sorted(events):
        if kind == "p":
            p_arrive(k)
            if k < FAR:
                p_step(k + 1)
            y_step(k)
        elif kind == "y":
            y_forward(k)
        elif kind == "q":
            for m in (0, 3, 1, 2):
                q_arrive(k, m)
                if k < FAR:
                    q_step(k + 1, m)
        else:
            if not ready:
                val_copy.wait()
                tab_copy.wait()
                ready = True
            y_far(k)
            messages(k)

    w_copy.wait()

    def project(c, into):
        def one(r, carry):
            for h in range(2):
                last = tab_s[3, (c * REL + r) * 2 + h]
                terms[c, r, pl.ds(h * BLOCK, BLOCK)] = chain[last].astype(BF16)
            into[...] += jnp.dot(terms[c, r], weight[r], preferred_element_type=F32)
            return carry

        into[...] = jnp.zeros_like(into)
        lax.fori_loop(0, REL, one, 0)

    def blocks(body, low, n):
        def one(b, carry):
            body(pl.ds(pl.multiple_of(low + b * 32, 32), 32))
            return carry

        lax.fori_loop(0, n // 32, one, 0)

    halves = [pl.ds(h * BLOCK, BLOCK) for h in range(2)]

    panels = [x_at(2), x_at(-turn), x_at(turn), s]
    partner_panels = [x_at(2), x_at(turn), x_at(-turn), s]
    ahead, behind = x_dev(turn), x_dev(-turn)
    swaps, moves = [], []

    def combine(i):
        swaps[i].wait_recv()
        copies = []
        for h in range(2):
            if i == 2:
                moves[0][h].wait_recv()

            def one(part):
                value = keep[i, part] + ex[i, part].astype(F32)
                if i == 2:
                    value = value + cr[0, part].astype(F32)
                cs[i, part] = value.astype(BF16)

            blocks(one, h * BLOCK, BLOCK)
            copies.append(go(remote(cs.at[i, halves[h]], cr.at[i, halves[h]], cx_s.at[i, h], cx_r.at[i, h],
                                    behind if i == 1 else ahead)))
        moves.append(copies)

    for i in range(4):
        project(partner_panels[i] * 2 + 1 - g, work)

        def narrow(part):
            give[i, part] = work[part].astype(BF16)

        blocks(narrow, 0, 2 * BLOCK)
        if i > 0:
            combine(i - 1)
        project(panels[i] * 2 + g, keep.at[i])
        swaps.append(go(remote(give.at[i], ex.at[i], ex_s.at[i], ex_r.at[i], partner)))
    swaps[3].wait_recv()
    own = s * 2 + g

    def activate(part):
        value = keep[3, part] + ex[3, part].astype(F32) + cr[1, part].astype(F32) + cr[2, part].astype(F32)
        logistic = 1.0 / (1.0 + jnp.exp(-value))
        result[part] = (value * logistic).astype(BF16)
        slope = logistic * (1.0 + value * (1.0 - logistic))
        rows[own, part] = (cot[part].astype(F32) * slope).astype(BF16)

    def share(c, sem, to, h):
        ref = rows.at[c, halves[h]]
        return go(remote(ref, ref, gx_s.at[sem, h], gx_r.at[sem, h], to))

    def relay(c, sem, h):
        ref = rows.at[c, halves[h]]
        return go(remote(ref, ref, gp_s.at[sem, h], gp_r.at[sem, h], partner))

    gx0, gx1, gx2, gp0, gp1, gp2, gp3 = [], [], [], [], [], [], []
    for h in range(2):
        moves[1][h].wait_recv()
        moves[2][h].wait_recv()
        blocks(activate, h * BLOCK, BLOCK)
        gx0.append(share(own, 0, ahead, h))
        gx1.append(share(own, 1, behind, h))
        gp0.append(relay(own, 0, h))

    def wait_both(copies):
        for copy in copies:
            copy.wait_recv()

    out_copy = pltpu.make_async_copy(result, out, out_sem.at[0])
    out_copy.start()

    def add_terms(c, first=False):
        def one(r, carry):
            product = lax.dot_general(terms[c, r], rows[c], (((0,), (0,)), ((), ())),
                                      preferred_element_type=F32)
            if first:
                acc[r] = product
            else:
                acc[r] = acc[r] + product
            return carry

        lax.fori_loop(0, REL, one, 0)

    add_terms(own, first=True)
    wait_both(gp0)
    add_terms(s * 2 + 1 - g)
    from_behind, from_ahead, from_far = x_at(-turn) * 2 + g, x_at(turn) * 2 + g, x_at(2) * 2 + g
    for h in range(2):
        gx0[h].wait_recv()
        gx2.append(share(from_behind, 2, ahead, h))
        gp1.append(relay(from_behind, 1, h))
    for h in range(2):
        gx1[h].wait_recv()
        gp2.append(relay(from_ahead, 2, h))
    add_terms(from_behind)
    add_terms(from_ahead)
    wait_both(gp1)
    add_terms(x_at(turn) * 2 + 1 - g)
    wait_both(gp2)
    add_terms(x_at(-turn) * 2 + 1 - g)
    for h in range(2):
        gx2[h].wait_recv()
        gp3.append(relay(from_far, 3, h))
    add_terms(from_far)
    wait_both(gp3)
    add_terms(x_at(2) * 2 + 1 - g)

    def ring_sum(load, stage, got, ss, rs, lane, pos, dev):
        copies = {}

        def put(k, p, to, r):
            value = load(r, p)
            if k == 2:
                copies[0, r].wait_recv()
                value = value + got[0, r].astype(F32)
            stage[k, r] = value.astype(BF16)
            copies[k, r] = go(remote(stage.at[k, r], got.at[k, r], ss.at[lane, k, r], rs.at[lane, k, r], to))

        def end(r):
            copies[1, r].wait_recv()
            copies[2, r].wait_recv()
            return load(r, pos(0)) + got[1, r].astype(F32) + got[2, r].astype(F32)

        return (lambda r: put(0, pos(2), dev(turn), r), lambda r: put(1, pos(-turn), dev(-turn), r),
                lambda r: put(2, pos(turn), dev(turn), r), end)

    def both(one, two, n, store=None):
        for phase in range(3):
            for r in range(n):
                one[phase](r)
                two[phase](r)
        for r in range(n):
            value_a, value_b = one[3](r), two[3](r)
            if store is not None:
                store[0](r, value_a)
                store[1](r, value_b)

    def into_a(r, value):
        a_sum[r] = value

    def into_b(r, value):
        b_sum[r] = value

    def into_tail_a(r, value):
        tail[r] = value

    def into_tail_b(r, value):
        tail[3 + r] = value

    both(ring_sum(lambda r, p: acc[r, pl.ds(p * 64, 64)], a_send, a_recv, s1_s, s1_r, 0, x_at, x_dev),
         ring_sum(lambda r, p: acc[3 + r, pl.ds(p * 64, 64)], b_send, b_recv, s1_s, s1_r, 1, y_at, y_dev),
         3, (into_a, into_b))
    both(ring_sum(lambda r, p: a_sum[r, pl.ds(p * 16, 16)], a2_send, a2_recv, s2_s, s2_r, 0, y_at, y_dev),
         ring_sum(lambda r, p: b_sum[r, pl.ds(p * 16, 16)], b2_send, b2_recv, s2_s, s2_r, 1, x_at, x_dev),
         3, (into_tail_a, into_tail_b))
    for j in range(NZ):
        for r in range(REL):
            for h in range(2):
                z_rows[j, pl.ds(2 * r + h, 1)] = tail[r, pl.ds(j, 1), pl.ds(h * BLOCK, BLOCK)]
    z_send[...] = z_rows[...].astype(BF16)
    third = []
    for d in range(1, NZ):
        to = (z + d) % NZ
        third.append(go(remote(z_send.at[to], z_recv.at[d], z1_s.at[d], z1_r.at[d], z_dev(d))))
    value = z_rows[z]
    for d in range(1, NZ):
        third[d - 1].wait_recv()
        value = value + z_recv[d].astype(F32)
    z_full[z] = value.astype(BF16)

    fourth = []
    for d in range(1, NZ):
        fourth.append(go(remote(z_full.at[z], z_full.at[z], z2_s.at[d], z2_r.at[d], z_dev(d))))
    for copy in fourth:
        copy.wait_recv()
    z_rows[...] = z_full[...].astype(F32)
    for j in range(NZ):
        for r in range(REL):
            for h in range(2):
                tail[r, pl.ds(j, 1), pl.ds(h * BLOCK, BLOCK)] = z_rows[j, pl.ds(2 * r + h, 1)]
    for r in range(3):
        a_all[s, y, r] = tail[r].astype(BF16)
        b_all[y, s, r] = tail[3 + r].astype(BF16)

    def ring_spread(ref, ss, rs, lane, pos, dev):
        copies = {}

        def put(k, p, to, t):
            if k == 2:
                copies[0, t].wait_recv()
            copies[k, t] = go(remote(ref(p, t), ref(p, t), ss.at[lane, k, t], rs.at[lane, k, t], to))

        def end(t):
            copies[1, t].wait_recv()
            copies[2, t].wait_recv()

        return (lambda t: put(0, pos(0), dev(turn), t), lambda t: put(1, pos(0), dev(-turn), t),
                lambda t: put(2, pos(-turn), dev(turn), t), end)

    both(ring_spread(lambda p, t: a_all.at[s, p], s4_s, s4_r, 0, y_at, y_dev),
         ring_spread(lambda p, t: b_all.at[y, p], s4_s, s4_r, 1, x_at, x_dev), 1)
    both(ring_spread(lambda p, t: a_all.at[p, t], s5_s, s5_r, 0, x_at, x_dev),
         ring_spread(lambda p, t: b_all.at[p, t], s5_s, s5_r, 1, y_at, y_dev), 4)
    a_copy = pltpu.make_async_copy(a_all, a_out, out_sem.at[1])
    b_copy = pltpu.make_async_copy(b_all, b_out, out_sem.at[2])
    a_copy.start()
    b_copy.start()
    for copy in sent:
        copy.wait_send()
    out_copy.wait()
    a_copy.wait()
    b_copy.wait()


def layer(source_feats, table, pick, count, values, weight, cotangent):
    hbm = pl.BlockSpec(memory_space=pl.ANY)
    vmem = pl.BlockSpec(memory_space=pltpu.VMEM)
    smem = pl.BlockSpec(memory_space=pltpu.SMEM)
    dma = pltpu.SemaphoreType.DMA
    V = pltpu.VMEM
    steps = FAR + 1
    slots = values.shape[0]
    sums = jax.ShapeDtypeStruct((4, 4, 3, 16, D), BF16)
    return pl.pallas_call(
        layer_kernel,
        out_shape=(jax.ShapeDtypeStruct((2 * BLOCK, D), BF16), sums, sums),
        in_specs=[hbm, vmem, vmem, smem, hbm, hbm, vmem],
        out_specs=(hbm, hbm, hbm),
        scratch_shapes=[
            V((PARTS, 2, BLOCK, D), BF16), V((NZ, NY, BLOCK, D), BF16),
            V((NZ, ROWS_P, D), BF16), V((NZ, ROWS_P, D), BF16), V((NZ, ROWS_P, D), BF16),
            V((NZ, HALF_P, D), BF16), V((NZ, HALF_P, D), BF16),
            V((8, BLOCK), I32), V((3, 8, BLOCK), I32), pltpu.SMEM((3, 8, BLOCK), I32),
            V((slots, BLOCK, BLOCK), BF16), V((REL, D, D), BF16),
            V((PARTS + 1, BLOCK, D), F32), V((8, BLOCK), I32), pltpu.SMEM((8, BLOCK), I32),
            V((CHUNKS, REL, 256, D), BF16), V((256, D), F32), V((4, 256, D), F32), V((4, 256, D), BF16),
            V((4, 256, D), BF16), V((3, 256, D), BF16), V((3, 256, D), BF16), V((CHUNKS, 256, D), BF16),
            V((REL, D, D), F32),
            V((256, D), BF16), V((4, 4, 3, 16, D), BF16), V((4, 4, 3, 16, D), BF16),
            V((3, 3, 64, D), BF16), V((3, 3, 64, D), BF16), V((3, 3, 64, D), BF16), V((3, 3, 64, D), BF16),
            V((3, 64, D), F32), V((3, 64, D), F32),
            V((3, 3, 16, D), BF16), V((3, 3, 16, D), BF16), V((3, 3, 16, D), BF16), V((3, 3, 16, D), BF16),
            V((REL, 16, D), F32), V((NZ, 16, BLOCK), F32), V((NZ, 16, BLOCK), BF16),
            V((NZ, 16, BLOCK), BF16), V((NZ, 16, BLOCK), BF16),
            dma, dma, dma, dma, dma((3,)), dma, dma((3,)), dma((3,))]
        + [dma((NZ,))] * 4
        + [dma((steps,))] * 4 + [dma((NZ,))] * 8 + [dma((3,))] * 2 + [dma((steps, NY))] * 4
        + [dma((4,))] * 2 + [dma((3, 2))] * 2 + [dma((3, 2))] * 2 + [dma((4, 2))] * 2
        + [dma((2, 3, 3))] * 4 + [dma((NZ,))] * 4 + [dma((2, 3, 4))] * 4,
        compiler_params=pltpu.CompilerParams(
            collective_id=0, has_side_effects=True, vmem_limit_bytes=60 << 20),
        name="layer",
    )(source_feats, table, pick, count, values, weight, cotangent)


def finish_kernel(result, a_all, b_all, out, grad):
    out[...] = result[...]
    for i in range(4):
        for j in range(4):
            part = pl.ds(64 * i + 16 * j, 16)
            for r in range(3):
                grad[r, part] = a_all[i, j, r].astype(F32)
                grad[3 + r, part] = b_all[i, j, r].astype(F32)


def finish(result, a_all, b_all):
    vmem = pl.BlockSpec(memory_space=pltpu.VMEM)
    return pl.pallas_call(
        finish_kernel,
        out_shape=(jax.ShapeDtypeStruct((2 * BLOCK, D), BF16),
                   jax.ShapeDtypeStruct((REL, D, D), F32)),
        in_specs=[vmem] * 3,
        out_specs=(vmem, vmem),
        name="finish",
    )(result, a_all, b_all)


def local(source_feats, rel_weight, halo_pick, entry_index, entry_count, entry_values, cotangent):
    slots = entry_index.shape[-1]
    return finish(*layer(
        source_feats.reshape(2, BLOCK, D), entry_index.reshape(3, 1, slots), halo_pick.reshape(1, -1), entry_count.reshape(1),
        entry_values.reshape(slots, BLOCK, BLOCK), rel_weight, cotangent))


def solution(mesh):
    return jax.shard_map(
        local,
        mesh=mesh,
        in_specs=(
            P(("dom", "src", "rel"), None),
            P("rel", None, None),
            P("dom", "src", "rel", None),
            P("dom", "src", "rel", None, None),
            P("dom", "src", "rel"),
            P("dom", "src", "rel", None, None, None),
            P(("dom", "src", "rel"), None),
        ),
        out_specs=(P(("dom", "src", "rel"), None), P("rel", None, None)),
        check_vma=False,
    )
```

```python
import jax
import jax.numpy as jnp
from jax import lax
from jax.experimental import pallas as pl
from jax.experimental.pallas import tpu as pltpu
from jax.sharding import PartitionSpec as P

MESH = pl.DeviceIdType.MESH
F32 = jnp.float32
BF16 = jnp.bfloat16
I32 = jnp.int32

NY = 4
NZ = 16
NX = 4
PARTS = 64
BLOCK = 128
D = 256
REL = 6
CHUNKS = 8
SLOTS = CHUNKS * REL * 2
ROWS_P = 96
HALF_P = 48
ROWS_Q = 32
HALF_Q = 16
FAR = NZ // 2

TIME_P = [5.0 * k for k in range(FAR + 1)]
TIME_Q = [5.0 * k + 1.0 for k in range(FAR + 1)]
TIME_Y = [5.0 * k + 6.0 for k in range(FAR)] + [5.0 * FAR + 1.2]
MESSAGE_LAG = 8.5


def remote(src, dst, send_sem, recv_sem, to):
    return pltpu.make_async_remote_copy(
        src_ref=src, dst_ref=dst, send_sem=send_sem, recv_sem=recv_sem,
        device_id=to, device_id_type=MESH)


def choose(second, one, zero):
    return jnp.where(second == 1, one, zero)


def offsets(k):
    if k == 0:
        return [(0, 0)]
    if k == FAR:
        return [(2 * k - 1, k)]
    return [(2 * k - 1, -k), (2 * k, k)]


def layer_kernel(src, table, pick, count, values_hbm, weight_hbm, cot,
                 out, a_out, b_out,
                 held, got, stage_up, stage_down, stage_far, relay_up, relay_down, my_pick, peer_pick, peer_s,
                 values, weight, chain, tab, tab_s, terms, work, keep, give, ex, cs, cr, rows, acc,
                 result, a_all, b_all,
                 a_send, a_recv, b_send, b_recv, a_sum, b_sum,
                 a2_send, a2_recv, b2_send, b2_recv, tail, z_rows, z_send, z_recv, z_full,
                 own_sem, val_sem, w_sem, tab_sem, out_sem, pick_sem, pp_s, pp_r, hu_s, hu_r, hd_s, hd_r,
                 pf_s, pf_r, pb_s, pb_r, yf_s, yf_r, yb_s, yb_r,
                 ff_s, ff_r, fb_s, fb_r, q0_s, q0_r, qf_s, qf_r, qb_s, qb_r,
                 ex_s, ex_r, cx_s, cx_r, gx_s, gx_r, gp_s, gp_r,
                 s1_s, s1_r, s2_s, s2_r, z1_s, z1_r, z2_s, z2_r, s4_s, s4_r, s5_s, s5_r):
    dom, s, g = lax.axis_index("dom"), lax.axis_index("src"), lax.axis_index("rel")
    z, y = dom // NY, dom % NY
    turn = 1 - 2 * g
    partner = {"rel": 1 - g}

    def at(zo, yo):
        return ((z + zo + NZ) % NZ) * NY + (y + yo + NY) % NY

    def x_at(o):
        return (s + o + NX) % NX

    def y_at(o):
        return (y + o + NY) % NY

    def x_dev(o):
        return {"src": x_at(o)}

    def y_dev(o):
        return {"dom": z * NY + y_at(o)}

    def z_dev(o):
        return {"dom": ((z + o + NZ) % NZ) * NY + y}

    own_copy = pltpu.make_async_copy(src, held.at[dom], own_sem)
    own_copy.start()
    val_copy = pltpu.make_async_copy(values_hbm, values, val_sem)
    val_copy.start()
    w_copy = pltpu.make_async_copy(weight_hbm, weight, w_sem)
    w_copy.start()

    near = [partner, x_dev(1), x_dev(-1), y_dev(1), y_dev(-1), y_dev(2), z_dev(1), z_dev(-1)]
    barrier = pltpu.get_barrier_semaphore()
    for to in near:
        pl.semaphore_signal(barrier, inc=1, device_id=to, device_id_type=MESH)
    my_pick[...] = jnp.zeros_like(my_pick)
    my_pick[0:1, 0:PARTS] = pick[...]
    own_copy.wait()
    pl.semaphore_wait(barrier, len(near))

    sent = []

    def go(copy):
        copy.start()
        sent.append(copy)
        return copy

    def send(where, row, n, s_sem, r_sem, to):
        ref = held.at[at(*where), :, pl.ds(row, n)]
        go(remote(ref, ref, s_sem, r_sem, to))

    def arrive(where, row, n, s_sem, r_sem):
        ref = held.at[at(*where), :, pl.ds(row, n)]
        remote(ref, ref, s_sem, r_sem, z_dev(1)).wait_recv()

    def cut(k, low, full, half, back):
        if k < FAR:
            return low, full
        return low + (half if back else 0), half

    def p_step(k):
        send((-(k - 1), 0), *cut(k, 0, ROWS_P, HALF_P, False), pf_s.at[k], pf_r.at[k], z_dev(1))
        send((k - 1, 0), *cut(k, 0, ROWS_P, HALF_P, True), pb_s.at[k], pb_r.at[k], z_dev(-1))

    def p_arrive(k):
        arrive((-k, 0), *cut(k, 0, ROWS_P, HALF_P, False), pf_s.at[k], pf_r.at[k])
        arrive((k, 0), *cut(k, 0, ROWS_P, HALF_P, True), pb_s.at[k], pb_r.at[k])

    def q_step(k, m):
        send((-(k - 1), m), *cut(k, ROWS_P, ROWS_Q, HALF_Q, False), qf_s.at[k, m], qf_r.at[k, m], z_dev(1))
        send((k - 1, m), *cut(k, ROWS_P, ROWS_Q, HALF_Q, True), qb_s.at[k, m], qb_r.at[k, m], z_dev(-1))

    def q_arrive(k, m):
        arrive((-k, m), *cut(k, ROWS_P, ROWS_Q, HALF_Q, False), qf_s.at[k, m], qf_r.at[k, m])
        arrive((k, m), *cut(k, ROWS_P, ROWS_Q, HALF_Q, True), qb_s.at[k, m], qb_r.at[k, m])

    def y_step(k):
        for j, zo in offsets(k):
            q = at(zo, 0)
            top = pl.ds(0, ROWS_P)
            stage_far[j] = choose(peer_s[2, 0, q], held[q, 1, top], held[q, 0, top])
            stage_up[j] = choose(peer_s[0, 0, q], held[q, 1, top], held[q, 0, top])
            stage_down[j] = choose(peer_s[1, 0, q], held[q, 1, top], held[q, 0, top])
            go(remote(stage_far.at[j, pl.ds(0, HALF_P)], relay_up.at[j], hu_s.at[j], hu_r.at[j], y_dev(1)))
            go(remote(stage_far.at[j, pl.ds(HALF_P, HALF_P)], relay_down.at[j], hd_s.at[j], hd_r.at[j], y_dev(-1)))
            go(remote(stage_up.at[j], got.at[j, 3, top], yf_s.at[j], yf_r.at[j], y_dev(1)))
            go(remote(stage_down.at[j], got.at[j, 1, top], yb_s.at[j], yb_r.at[j], y_dev(-1)))

    def landed(ref, s_sem, r_sem):
        remote(ref, ref, s_sem, r_sem, y_dev(1)).wait_recv()

    def y_forward(k):
        for j, zo in offsets(k):
            landed(relay_up.at[j], hu_s.at[j], hu_r.at[j])
            go(remote(relay_up.at[j], got.at[j, 2, pl.ds(0, HALF_P)], ff_s.at[j], ff_r.at[j], y_dev(1)))
            landed(relay_down.at[j], hd_s.at[j], hd_r.at[j])
            go(remote(relay_down.at[j], got.at[j, 2, pl.ds(HALF_P, HALF_P)], fb_s.at[j], fb_r.at[j], y_dev(-1)))

    def y_far(k):
        for j, zo in offsets(k):
            landed(got.at[j, 3, pl.ds(0, ROWS_P)], yf_s.at[j], yf_r.at[j])
            landed(got.at[j, 1, pl.ds(0, ROWS_P)], yb_s.at[j], yb_r.at[j])
            landed(got.at[j, 2, pl.ds(0, HALF_P)], ff_s.at[j], ff_r.at[j])
            landed(got.at[j, 2, pl.ds(HALF_P, HALF_P)], fb_s.at[j], fb_r.at[j])

    def message(i, zo, m):
        j = i * NY + m
        e, before, second = tab_s[0, j], tab_s[1, j], tab_s[2, j]
        q = at(zo, m)
        if m == 0:
            block = choose(second, held[q, 1], held[q, 0])
        else:
            rest = pl.ds(ROWS_P, ROWS_Q)
            block = jnp.concatenate(
                [got[i, m, pl.ds(0, ROWS_P)], choose(second, held[q, 1, rest], held[q, 0, rest])], axis=0)
        product = jnp.dot(values[e], block, preferred_element_type=F32)
        chain[j] = product + chain[before]

    def messages(k):
        for i, zo in offsets(k):
            for m in range(NY):
                message(i, zo, m)

    p_step(1)
    swaps_of_picks = []
    for i, o in enumerate((1, -1, 2)):
        there = (1, 0, 2)[i]
        swaps_of_picks.append(go(remote(my_pick, peer_pick.at[there], pp_s.at[i], pp_r.at[there], y_dev(o))))
    send((0, 0), ROWS_P, ROWS_Q, q0_s.at[0], q0_r.at[0], y_dev(1))
    send((0, 0), ROWS_P, ROWS_Q, q0_s.at[1], q0_r.at[1], y_dev(-1))
    send((0, 0), ROWS_P, ROWS_Q, q0_s.at[2], q0_r.at[2], y_dev(2))
    q_step(1, 0)

    for i in range(3):
        landed(peer_pick.at[i], pp_s.at[i], pp_r.at[i])
    pick_copy = pltpu.make_async_copy(peer_pick, peer_s, pick_sem)
    pick_copy.start()
    pick_copy.wait()
    y_step(0)

    arrive((0, -1), ROWS_P, ROWS_Q, q0_s.at[0], q0_r.at[0])
    q_step(1, 3)
    arrive((0, 1), ROWS_P, ROWS_Q, q0_s.at[1], q0_r.at[1])
    q_step(1, 1)
    arrive((0, 2), ROWS_P, ROWS_Q, q0_s.at[2], q0_r.at[2])
    q_step(1, 2)

    lanes = lax.broadcasted_iota(I32, (PARTS, PARTS), 1)
    subs = lax.broadcasted_iota(I32, (PARTS, PARTS), 0)

    def as_column(row):
        return jnp.sum(jnp.where(lanes == subs, row, 0), axis=1, keepdims=True)

    def as_row(column):
        return jnp.sum(jnp.where(lanes == subs, column, 0), axis=0, keepdims=True)

    index = subs[:, :1]
    step = index // NY
    z_off = jnp.where(step % 2 == 1, -((step + 1) // 2), step // 2)
    part = ((z + z_off + NZ) % NZ) * NY + (y + index % NY) % NY
    entry = lanes[:1, :]
    slot_of = (table[0] // 2 * REL + table[2]) * 2 + table[0] % 2
    slot_of = jnp.where(entry < count[0], slot_of, SLOTS + entry)
    reads = jnp.where(table[1] == part, 1, 0)
    entry_at = jnp.max(reads * entry, axis=1, keepdims=True)
    slot_at = jnp.max(reads * slot_of, axis=1, keepdims=True)
    pick_at = jnp.sum(jnp.where(entry == part, pick[...], 0), axis=1, keepdims=True)
    slot_row = as_row(slot_at)
    earlier = jnp.max(jnp.where((slot_row == slot_at) & (lanes < subs), lanes, -1), axis=1, keepdims=True)
    earlier = jnp.where(earlier < 0, PARTS, earlier)
    tab[...] = jnp.zeros_like(tab)
    tab[0:1, 0:PARTS] = as_row(entry_at)
    tab[1:2, 0:PARTS] = as_row(earlier)
    tab[2:3, 0:PARTS] = as_row(pick_at)
    slot_lane = lax.broadcasted_iota(I32, (PARTS, BLOCK), 1)
    order = lax.broadcasted_iota(I32, (PARTS, BLOCK), 0)
    final = jnp.max(jnp.where(slot_at == slot_lane, order, -1), axis=0, keepdims=True)
    tab[3:4, :] = jnp.where(final < 0, PARTS, final)
    chain[PARTS] = jnp.zeros((BLOCK, D), F32)

    tab_copy = pltpu.make_async_copy(tab, tab_s, tab_sem)
    tab_copy.start()
    z_rows[...] = jnp.zeros_like(z_rows)

    events = []
    for k in range(FAR + 1):
        if k > 0:
            events.append((TIME_P[k], 0, k, "p"))
            events.append((TIME_Q[k], 2, k, "q"))
        events.append((max(TIME_Y[k], TIME_P[k] + 0.1), 1, k, "y"))
        events.append((max(TIME_Y[k] + MESSAGE_LAG, TIME_Q[k] + 0.1), 3, k, "m"))
    ready = False
    for _, _, k, kind in sorted(events):
        if kind == "p":
            p_arrive(k)
            if k < FAR:
                p_step(k + 1)
            y_step(k)
        elif kind == "y":
            y_forward(k)
        elif kind == "q":
            for m in (0, 3, 1, 2):
                q_arrive(k, m)
                if k < FAR:
                    q_step(k + 1, m)
        else:
            if not ready:
                val_copy.wait()
                tab_copy.wait()
                ready = True
            y_far(k)
            messages(k)

    w_copy.wait()

    def project(c, into):
        def one(r, carry):
            for h in range(2):
                last = tab_s[3, (c * REL + r) * 2 + h]
                terms[c, r, pl.ds(h * BLOCK, BLOCK)] = chain[last].astype(BF16)
            into[...] += jnp.dot(terms[c, r], weight[r], preferred_element_type=F32)
            return carry

        into[...] = jnp.zeros_like(into)
        lax.fori_loop(0, REL, one, 0)

    def blocks(body, low, n):
        def one(b, carry):
            body(pl.ds(pl.multiple_of(low + b * 32, 32), 32))
            return carry

        lax.fori_loop(0, n // 32, one, 0)

    halves = [pl.ds(h * BLOCK, BLOCK) for h in range(2)]

    panels = [x_at(2), x_at(-turn), x_at(turn), s]
    partner_panels = [x_at(2), x_at(turn), x_at(-turn), s]
    ahead, behind = x_dev(turn), x_dev(-turn)
    swaps, moves = [], []

    def combine(i):
        swaps[i].wait_recv()
        copies = []
        for h in range(2):
            if i == 2:
                moves[0][h].wait_recv()

            def one(part):
                value = keep[i, part] + ex[i, part].astype(F32)
                if i == 2:
                    value = value + cr[0, part].astype(F32)
                cs[i, part] = value.astype(BF16)

            blocks(one, h * BLOCK, BLOCK)
            copies.append(go(remote(cs.at[i, halves[h]], cr.at[i, halves[h]], cx_s.at[i, h], cx_r.at[i, h],
                                    behind if i == 1 else ahead)))
        moves.append(copies)

    for i in range(4):
        project(partner_panels[i] * 2 + 1 - g, work)

        def narrow(part):
            give[i, part] = work[part].astype(BF16)

        blocks(narrow, 0, 2 * BLOCK)
        if i > 0:
            combine(i - 1)
        swaps.append(go(remote(give.at[i], ex.at[i], ex_s.at[i], ex_r.at[i], partner)))
        project(panels[i] * 2 + g, keep.at[i])
    swaps[3].wait_recv()
    own = s * 2 + g

    def activate(part):
        value = keep[3, part] + ex[3, part].astype(F32) + cr[1, part].astype(F32) + cr[2, part].astype(F32)
        logistic = 1.0 / (1.0 + jnp.exp(-value))
        result[part] = (value * logistic).astype(BF16)
        slope = logistic * (1.0 + value * (1.0 - logistic))
        rows[own, part] = (cot[part].astype(F32) * slope).astype(BF16)

    def share(c, sem, to, h):
        ref = rows.at[c, halves[h]]
        return go(remote(ref, ref, gx_s.at[sem, h], gx_r.at[sem, h], to))

    def relay(c, sem, h):
        ref = rows.at[c, halves[h]]
        return go(remote(ref, ref, gp_s.at[sem, h], gp_r.at[sem, h], partner))

    gx0, gx1, gx2, gp0, gp1, gp2, gp3 = [], [], [], [], [], [], []
    for h in range(2):
        moves[1][h].wait_recv()
        moves[2][h].wait_recv()
        blocks(activate, h * BLOCK, BLOCK)
        gx0.append(share(own, 0, ahead, h))
        gx1.append(share(own, 1, behind, h))
        gp0.append(relay(own, 0, h))

    def wait_both(copies):
        for copy in copies:
            copy.wait_recv()

    out_copy = pltpu.make_async_copy(result, out, out_sem.at[0])
    out_copy.start()

    def add_terms(c, first=False):
        def one(r, carry):
            product = lax.dot_general(terms[c, r], rows[c], (((0,), (0,)), ((), ())),
                                      preferred_element_type=F32)
            if first:
                acc[r] = product
            else:
                acc[r] = acc[r] + product
            return carry

        lax.fori_loop(0, REL, one, 0)

    add_terms(own, first=True)
    wait_both(gp0)
    add_terms(s * 2 + 1 - g)
    from_behind, from_ahead, from_far = x_at(-turn) * 2 + g, x_at(turn) * 2 + g, x_at(2) * 2 + g
    for h in range(2):
        gx0[h].wait_recv()
        gx2.append(share(from_behind, 2, ahead, h))
        gp1.append(relay(from_behind, 1, h))
    for h in range(2):
        gx1[h].wait_recv()
        gp2.append(relay(from_ahead, 2, h))
    add_terms(from_behind)
    add_terms(from_ahead)
    wait_both(gp1)
    add_terms(x_at(turn) * 2 + 1 - g)
    wait_both(gp2)
    add_terms(x_at(-turn) * 2 + 1 - g)
    for h in range(2):
        gx2[h].wait_recv()
        gp3.append(relay(from_far, 3, h))
    add_terms(from_far)
    wait_both(gp3)
    add_terms(x_at(2) * 2 + 1 - g)

    def ring_sum(load, stage, got, ss, rs, lane, pos, dev):
        copies = {}

        def put(k, p, to, r):
            value = load(r, p)
            if k == 2:
                copies[0, r].wait_recv()
                value = value + got[0, r].astype(F32)
            stage[k, r] = value.astype(BF16)
            copies[k, r] = go(remote(stage.at[k, r], got.at[k, r], ss.at[lane, k, r], rs.at[lane, k, r], to))

        def end(r):
            copies[1, r].wait_recv()
            copies[2, r].wait_recv()
            return load(r, pos(0)) + got[1, r].astype(F32) + got[2, r].astype(F32)

        return (lambda r: put(0, pos(2), dev(turn), r), lambda r: put(1, pos(-turn), dev(-turn), r),
                lambda r: put(2, pos(turn), dev(turn), r), end)

    def both(one, two, n, store=None):
        for phase in range(3):
            for r in range(n):
                one[phase](r)
                two[phase](r)
        for r in range(n):
            value_a, value_b = one[3](r), two[3](r)
            if store is not None:
                store[0](r, value_a)
                store[1](r, value_b)

    def into_a(r, value):
        a_sum[r] = value

    def into_b(r, value):
        b_sum[r] = value

    def into_tail_a(r, value):
        tail[r] = value

    def into_tail_b(r, value):
        tail[3 + r] = value

    both(ring_sum(lambda r, p: acc[r, pl.ds(p * 64, 64)], a_send, a_recv, s1_s, s1_r, 0, x_at, x_dev),
         ring_sum(lambda r, p: acc[3 + r, pl.ds(p * 64, 64)], b_send, b_recv, s1_s, s1_r, 1, y_at, y_dev),
         3, (into_a, into_b))
    both(ring_sum(lambda r, p: a_sum[r, pl.ds(p * 16, 16)], a2_send, a2_recv, s2_s, s2_r, 0, y_at, y_dev),
         ring_sum(lambda r, p: b_sum[r, pl.ds(p * 16, 16)], b2_send, b2_recv, s2_s, s2_r, 1, x_at, x_dev),
         3, (into_tail_a, into_tail_b))
    for j in range(NZ):
        for r in range(REL):
            for h in range(2):
                z_rows[j, pl.ds(2 * r + h, 1)] = tail[r, pl.ds(j, 1), pl.ds(h * BLOCK, BLOCK)]
    z_send[...] = z_rows[...].astype(BF16)
    third = []
    for d in range(1, NZ):
        to = (z + d) % NZ
        third.append(go(remote(z_send.at[to], z_recv.at[d], z1_s.at[d], z1_r.at[d], z_dev(d))))
    value = z_rows[z]
    for d in range(1, NZ):
        third[d - 1].wait_recv()
        value = value + z_recv[d].astype(F32)
    z_full[z] = value.astype(BF16)

    fourth = []
    for d in range(1, NZ):
        fourth.append(go(remote(z_full.at[z], z_full.at[z], z2_s.at[d], z2_r.at[d], z_dev(d))))
    for copy in fourth:
        copy.wait_recv()
    z_rows[...] = z_full[...].astype(F32)
    for j in range(NZ):
        for r in range(REL):
            for h in range(2):
                tail[r, pl.ds(j, 1), pl.ds(h * BLOCK, BLOCK)] = z_rows[j, pl.ds(2 * r + h, 1)]
    for r in range(3):
        a_all[s, y, r] = tail[r].astype(BF16)
        b_all[y, s, r] = tail[3 + r].astype(BF16)

    def ring_spread(ref, ss, rs, lane, pos, dev):
        copies = {}

        def put(k, p, to, t):
            if k == 2:
                copies[0, t].wait_recv()
            copies[k, t] = go(remote(ref(p, t), ref(p, t), ss.at[lane, k, t], rs.at[lane, k, t], to))

        def end(t):
            copies[1, t].wait_recv()
            copies[2, t].wait_recv()

        return (lambda t: put(0, pos(0), dev(turn), t), lambda t: put(1, pos(0), dev(-turn), t),
                lambda t: put(2, pos(-turn), dev(turn), t), end)

    both(ring_spread(lambda p, t: a_all.at[s, p], s4_s, s4_r, 0, y_at, y_dev),
         ring_spread(lambda p, t: b_all.at[y, p], s4_s, s4_r, 1, x_at, x_dev), 1)
    both(ring_spread(lambda p, t: a_all.at[p, t], s5_s, s5_r, 0, x_at, x_dev),
         ring_spread(lambda p, t: b_all.at[p, t], s5_s, s5_r, 1, y_at, y_dev), 4)
    a_copy = pltpu.make_async_copy(a_all, a_out, out_sem.at[1])
    b_copy = pltpu.make_async_copy(b_all, b_out, out_sem.at[2])
    a_copy.start()
    b_copy.start()
    for copy in sent:
        copy.wait_send()
    out_copy.wait()
    a_copy.wait()
    b_copy.wait()


def layer(source_feats, table, pick, count, values, weight, cotangent):
    hbm = pl.BlockSpec(memory_space=pl.ANY)
    vmem = pl.BlockSpec(memory_space=pltpu.VMEM)
    smem = pl.BlockSpec(memory_space=pltpu.SMEM)
    dma = pltpu.SemaphoreType.DMA
    V = pltpu.VMEM
    steps = FAR + 1
    slots = values.shape[0]
    sums = jax.ShapeDtypeStruct((4, 4, 3, 16, D), BF16)
    return pl.pallas_call(
        layer_kernel,
        out_shape=(jax.ShapeDtypeStruct((2 * BLOCK, D), BF16), sums, sums),
        in_specs=[hbm, vmem, vmem, smem, hbm, hbm, vmem],
        out_specs=(hbm, hbm, hbm),
        scratch_shapes=[
            V((PARTS, 2, BLOCK, D), BF16), V((NZ, NY, BLOCK, D), BF16),
            V((NZ, ROWS_P, D), BF16), V((NZ, ROWS_P, D), BF16), V((NZ, ROWS_P, D), BF16),
            V((NZ, HALF_P, D), BF16), V((NZ, HALF_P, D), BF16),
            V((8, BLOCK), I32), V((3, 8, BLOCK), I32), pltpu.SMEM((3, 8, BLOCK), I32),
            V((slots, BLOCK, BLOCK), BF16), V((REL, D, D), BF16),
            V((PARTS + 1, BLOCK, D), F32), V((8, BLOCK), I32), pltpu.SMEM((8, BLOCK), I32),
            V((CHUNKS, REL, 256, D), BF16), V((256, D), F32), V((4, 256, D), F32), V((4, 256, D), BF16),
            V((4, 256, D), BF16), V((3, 256, D), BF16), V((3, 256, D), BF16), V((CHUNKS, 256, D), BF16),
            V((REL, D, D), F32),
            V((256, D), BF16), V((4, 4, 3, 16, D), BF16), V((4, 4, 3, 16, D), BF16),
            V((3, 3, 64, D), BF16), V((3, 3, 64, D), BF16), V((3, 3, 64, D), BF16), V((3, 3, 64, D), BF16),
            V((3, 64, D), F32), V((3, 64, D), F32),
            V((3, 3, 16, D), BF16), V((3, 3, 16, D), BF16), V((3, 3, 16, D), BF16), V((3, 3, 16, D), BF16),
            V((REL, 16, D), F32), V((NZ, 16, BLOCK), F32), V((NZ, 16, BLOCK), BF16),
            V((NZ, 16, BLOCK), BF16), V((NZ, 16, BLOCK), BF16),
            dma, dma, dma, dma, dma((3,)), dma, dma((3,)), dma((3,))]
        + [dma((NZ,))] * 4
        + [dma((steps,))] * 4 + [dma((NZ,))] * 8 + [dma((3,))] * 2 + [dma((steps, NY))] * 4
        + [dma((4,))] * 2 + [dma((3, 2))] * 2 + [dma((3, 2))] * 2 + [dma((4, 2))] * 2
        + [dma((2, 3, 3))] * 4 + [dma((NZ,))] * 4 + [dma((2, 3, 4))] * 4,
        compiler_params=pltpu.CompilerParams(
            collective_id=0, has_side_effects=True, vmem_limit_bytes=60 << 20),
        name="layer",
    )(source_feats, table, pick, count, values, weight, cotangent)


def finish_kernel(result, a_all, b_all, out, grad):
    out[...] = result[...]
    for i in range(4):
        for j in range(4):
            part = pl.ds(64 * i + 16 * j, 16)
            for r in range(3):
                grad[r, part] = a_all[i, j, r].astype(F32)
                grad[3 + r, part] = b_all[i, j, r].astype(F32)


def finish(result, a_all, b_all):
    vmem = pl.BlockSpec(memory_space=pltpu.VMEM)
    return pl.pallas_call(
        finish_kernel,
        out_shape=(jax.ShapeDtypeStruct((2 * BLOCK, D), BF16),
                   jax.ShapeDtypeStruct((REL, D, D), F32)),
        in_specs=[vmem] * 3,
        out_specs=(vmem, vmem),
        name="finish",
    )(result, a_all, b_all)


def local(source_feats, rel_weight, halo_pick, entry_index, entry_count, entry_values, cotangent):
    slots = entry_index.shape[-1]
    return finish(*layer(
        source_feats.reshape(2, BLOCK, D), entry_index.reshape(3, 1, slots), halo_pick.reshape(1, -1), entry_count.reshape(1),
        entry_values.reshape(slots, BLOCK, BLOCK), rel_weight, cotangent))


def solution(mesh):
    return jax.shard_map(
        local,
        mesh=mesh,
        in_specs=(
            P(("dom", "src", "rel"), None),
            P("rel", None, None),
            P("dom", "src", "rel", None),
            P("dom", "src", "rel", None, None),
            P("dom", "src", "rel"),
            P("dom", "src", "rel", None, None, None),
            P(("dom", "src", "rel"), None),
        ),
        out_specs=(P(("dom", "src", "rel"), None), P("rel", None, None)),
        check_vma=False,
    )
```
